32 devices in a mesh: space: 16 (over z, x, core), win: 2 (over y).
Axes of the slice: x: 2, y: 2, z: 4, core: 2. Of those that a mesh axis runs over, the one named last changes fastest.
Arguments:
- snapshots: bfloat16 [256, 3, 256, 128], P('win', None, 'space'), may hold values from -6 to 6
- metrics: float32 [4, 256, 128], P(None, 'space'), may hold values from -1.5 to 6
- range_test: bfloat16 [256, 64], P('win'), may hold values from -2 to 2
- corange_test: bfloat16 [64, 3, 256, 128], P(None, None, 'space'), may hold values from -0.01953125 to 0.01953125
Outputs:
- q_basis: float32 [256, 64, 3, 128], P(('space', 'win'))
- r_range: float32 [64, 64], replicated
- r_corange: float32 [64, 64], replicated
The draws below stay inside these ranges and needn't reach their ends.
All inputs are finite; a program needn't handle non-finite values.
Results may differ from the reference program's by a relative error of at most 0.0029.
Values may be sent and summed in bfloat16 or wider, within the bound.
No kernel may reach another device: no remote copies, remote signals or barrier semaphores. Data moves between devices by JAX's collectives and lax.ppermute only.
A program may use at most 64 MiB of HBM per device.

```python
import math
import jax
import jax.numpy as jnp
from jax import lax

K = 64
NY = 128
SNAP = 128
NX = 256
ALLSNAPS = 256
N_WIN = 2


def draw_metrics(key, part):
    subkeys = jax.random.split(key, 4)
    growth = 1.0 + 2.0 * jnp.arange(NX, dtype=jnp.float32)[:, None] / (NX - 1)
    stretch_x = jnp.exp(jax.random.uniform(subkeys[0], (NX, NY), jnp.float32, math.log(0.5), math.log(2.0)))
    stretch_y = jnp.exp(jax.random.uniform(subkeys[1], (NX, NY), jnp.float32, math.log(0.5), math.log(2.0)))
    skew_x = jnp.clip(0.25 * jax.random.normal(subkeys[2], (NX, NY), jnp.float32), -0.5, 0.5)
    skew_y = jnp.clip(0.25 * jax.random.normal(subkeys[3], (NX, NY), jnp.float32), -0.5, 0.5)
    return jnp.stack([growth * stretch_x, growth * skew_x, growth * skew_y, growth * stretch_y]).astype(jnp.float32)


def draw_range_test(key, part):
    subkeys = jax.random.split(key, 2)
    column_scale = jnp.exp(jax.random.uniform(subkeys[0], (K,), jnp.float32, math.log(0.3), math.log(3.0)))
    entries = jnp.clip(jax.random.normal(subkeys[1], (ALLSNAPS, K), jnp.float32), -4.0, 4.0)
    scaled = entries * column_scale[None, :] / jnp.sqrt(jnp.float32(ALLSNAPS))
    return jnp.clip(scaled, -2.0, 2.0).astype(jnp.bfloat16)


def levels(rng, shape, pieces, low, high):
    factor_of, own = 1.0, jax.random.fold_in(rng, 6)
    for dim, blocks in pieces:
        heights = jnp.exp(jax.random.uniform(jax.random.fold_in(own, dim), (blocks,), jnp.float32, low / len(pieces), high / len(pieces)))
        factor_of = factor_of * jnp.repeat(heights, shape[dim] // blocks).reshape([-1 if axis == dim else 1 for axis in range(len(shape))])
    return factor_of


def gaussian(stream_key, extent, width, most, cuts=(), held_as=jnp.bfloat16):
    values = jax.random.normal(stream_key, extent, jnp.float32) * width
    if len(cuts) > 0:
        values = levels(stream_key, extent, cuts, -0.22, 0.18) * values
    return jnp.clip(values, min=-most, max=most).astype(held_as)


def setup_inputs(seed: int = 0) -> dict:
    key_list = jax.random.split(jax.random.key(seed), 5)
    return {
        "snapshots": gaussian(key_list[0], (ALLSNAPS, 3, NX, NY), 1.0, 6.0, ((0, 2), (2, 16))),
        "metrics": draw_metrics(jax.random.fold_in(key_list[4], 71), 0),
        "range_test": draw_range_test(jax.random.fold_in(key_list[4], 71), 0),
        "corange_test": gaussian(key_list[3], (K, 3, NX, NY), (3 * NX * NY) ** -0.5, 0.01953125, ((2, 16),)),
    }


def derive(padded, metrics):
    values = padded.astype(jnp.float32)
    along_xi = (values[:, :, 2:, :] - values[:, :, :-2, :]) * 0.5
    center = values[:, :, 1:-1, :]
    wide = jnp.pad(center, ((0, 0), (0, 0), (0, 0), (1, 1)))
    along_eta = (wide[:, :, :, 2:] - wide[:, :, :, :-2]) * 0.5
    stretch_x = metrics[0]
    skew_x = metrics[1]
    skew_y = metrics[2]
    stretch_y = metrics[3]
    vortex = stretch_x * along_xi[:, 1] + skew_x * along_eta[:, 1] - skew_y * along_xi[:, 0] - stretch_y * along_eta[:, 0]
    press_x = stretch_x * along_xi[:, 2] + skew_x * along_eta[:, 2]
    press_y = skew_y * along_xi[:, 2] + stretch_y * along_eta[:, 2]
    return jnp.stack([vortex, press_x, press_y], axis=1).astype(jnp.bfloat16)

def upper_factor(gram):
    order = gram.shape[0]
    positions = jnp.arange(order, dtype=jnp.int32)

    def column_step(column, lower):
        onehot = (positions == column).astype(gram.dtype)
        row_now = jnp.dot(onehot, lower, precision=lax.Precision.HIGHEST)
        vector = jnp.dot(gram, onehot, precision=lax.Precision.HIGHEST) - jnp.dot(lower, row_now, precision=lax.Precision.HIGHEST)
        pivot = jnp.sqrt(jnp.sum(vector * onehot))
        filled = jnp.where(positions >= column, vector / pivot, jnp.zeros_like(vector))
        return lower + filled[:, None] * onehot[None, :]
    lower = lax.fori_loop(0, order, column_step, jnp.zeros_like(gram))
    return lower.T

def upper_inverse(upper):
    lower = upper.T
    order = lower.shape[0]
    positions = jnp.arange(order, dtype=jnp.int32)

    def row_step(row, solved):
        onehot = (positions == row).astype(lower.dtype)
        row_lower = jnp.dot(onehot, lower, precision=lax.Precision.HIGHEST)
        pivot = jnp.sum(row_lower * onehot)
        fresh = (onehot - jnp.dot(row_lower, solved, precision=lax.Precision.HIGHEST)) / pivot
        return solved + onehot[:, None] * fresh[None, :]
    solved = lax.fori_loop(0, order, row_step, jnp.zeros_like(lower))
    return solved.T

def reference(snapshots, metrics, range_test, corange_test):
    corange_wide = corange_test.astype(jnp.float32)

    def window(running, window_index):
        window_block = lax.dynamic_slice_in_dim(snapshots, window_index * SNAP, SNAP, 0)
        padded = jnp.pad(window_block, ((0, 0), (0, 0), (1, 1), (0, 0)))
        fields = derive(padded, metrics).astype(jnp.float32)
        test_block = lax.dynamic_slice_in_dim(range_test, window_index * SNAP, SNAP, 0).astype(jnp.float32)
        partial_sum = jnp.einsum('scxy,sk->xkcy', fields, test_block)
        projection = jnp.einsum('kcxy,scxy->ks', corange_wide, fields)
        window_gram = jnp.dot(projection, projection.T, precision=lax.Precision.HIGHEST)
        return (running + partial_sum, window_gram)
    initial = jnp.zeros((NX, K, 3, NY), jnp.float32)
    sketch, grams = lax.scan(window, initial, jnp.arange(N_WIN, dtype=jnp.int32))
    corange_gram = lax.optimization_barrier(jnp.sum(grams, axis=0)) / (N_WIN * SNAP)
    r_corange = upper_factor(corange_gram)
    range_gram = jnp.einsum('xkcy,xjcy->kj', sketch, sketch, precision=lax.Precision.HIGHEST) / (3 * NX * NY)
    r_range = upper_factor(range_gram)
    inverse = upper_inverse(r_range)
    q_basis = jnp.einsum('xkcy,kj->xjcy', sketch, inverse, precision=lax.Precision.HIGHEST)
    return (q_basis, r_range, r_corange)
```

```python
import jax
import jax.numpy as jnp
from jax import lax
from jax.experimental import pallas as pl
from jax.experimental.pallas import tpu as pltpu
from jax.sharding import PartitionSpec as P

BOTH = ("space", "win")
EXACT = lax.Precision.HIGHEST


def padded_2(value, sides, width):
    for axis, dim in sides:
        count, length = (lax.axis_size(axis), value.shape[dim])
        up = [(i, (i + 1) % count) for i in range(count - 1)]
        down = [(j, i) for i, j in up]
        last = lax.slice_in_dim(value, length - width, length, axis=dim)
        first = lax.slice_in_dim(value, 0, width, axis=dim)
        before = lax.ppermute(last, axis, up)
        after = lax.ppermute(first, axis, down)
        value = jnp.concatenate([before, value, after], axis=dim)
    return value


def derive(padded, metrics):
    values = padded.astype(jnp.float32)
    along_xi = (values[:, :, 2:, :] - values[:, :, :-2, :]) * 0.5
    center = values[:, :, 1:-1, :]
    wide = jnp.pad(center, ((0, 0), (0, 0), (0, 0), (1, 1)))
    along_eta = (wide[:, :, :, 2:] - wide[:, :, :, :-2]) * 0.5
    stretch_x = metrics[0]
    skew_x = metrics[1]
    skew_y = metrics[2]
    stretch_y = metrics[3]
    vortex = (
        stretch_x * along_xi[:, 1]
        + skew_x * along_eta[:, 1]
        - skew_y * along_xi[:, 0]
        - stretch_y * along_eta[:, 0]
    )
    press_x = stretch_x * along_xi[:, 2] + skew_x * along_eta[:, 2]
    press_y = skew_y * along_xi[:, 2] + stretch_y * along_eta[:, 2]
    return jnp.stack([vortex, press_x, press_y], axis=1).astype(jnp.bfloat16)


def hops(space, win):
    space_bits = [win << b for b in range(space.bit_length() - 1)]
    win_bits = [1 << b for b in range(win.bit_length() - 1)]
    stages = [space_bits[:1], win_bits[:1] + space_bits[1:2]]
    rest = win_bits[1:] + space_bits[2:]
    stages += [rest[i : i + 2] for i in range(0, len(rest), 2)]
    return [s for s in stages if s]


def total_over_all(value):
    space, win = lax.axis_size("space"), lax.axis_size("win")
    count = space * win
    if count & (count - 1) or win & (win - 1):
        return lax.psum(value, BOTH)
    for bits in hops(space, win):
        parts = {0: value}
        for b in bits:
            for mask in list(parts):
                pairs = [(i, i ^ mask ^ b) for i in range(count)]
                parts[mask ^ b] = lax.ppermute(value, BOTH, pairs)
        for b in bits:
            parts = {m: parts[m] + parts[m ^ b] for m in parts if not m & b}
        value = parts[0]
    return value


def eliminate(chains, step, save):
    order = chains[0].shape[0]
    for j in range(0, order, step):
        for m, matrix in enumerate(chains):
            cols = [jnp.broadcast_to(matrix[:, j + a : j + a + 1], matrix.shape) for a in range(step)]
            rows = [matrix[j + a : j + a + 1, :] for a in range(step)]
            top = j + step
            rest = matrix[top:, :]
            for a in range(step):
                pivot = cols[a][j + a : j + a + 1, :]
                scaled = rows[a] / pivot
                for c in range(a + 1, step):
                    ratio = cols[c][j + a : j + a + 1, :] / pivot
                    down = cols[a][j + c : j + c + 1, :]
                    cols[c] = cols[c] - cols[a] * ratio
                    rows[c] = rows[c] - scaled * down
                save(m, j + a, rows[a] * lax.rsqrt(pivot))
                if top < order:
                    rest = rest - cols[a][top:, :] * scaled
            if top < order:
                chains[m] = jnp.concatenate([matrix[:top, :], rest], axis=0)


def factor_kernel(range_ref, corange_ref, inverse_ref, r_range_ref, r_corange_ref, wide_r, wide_c):
    order = range_ref.shape[0]
    row = lax.broadcasted_iota(jnp.int32, (order, order), 0)
    col = lax.broadcasted_iota(jnp.int32, (order, order), 1)
    eye = (row == col).astype(jnp.float32)
    held = (wide_r, wide_c)

    def save(m, r, value):
        held[m][r : r + 1, :] = value

    chains = [jnp.concatenate([ref[...], eye], axis=1) for ref in (range_ref, corange_ref)]
    eliminate(chains, 8 if order % 8 == 0 else 1, save)
    r_range_ref[...] = jnp.where(col >= row, wide_r[:, :order], 0.0)
    r_corange_ref[...] = jnp.where(col >= row, wide_c[:, :order], 0.0)
    inverse_ref[...] = jnp.where(col <= row, wide_r[:, order:], 0.0)


def factors(range_gram, corange_gram):
    order = range_gram.shape[0]
    square = jax.ShapeDtypeStruct((order, order), jnp.float32)
    vmem = pl.BlockSpec(memory_space=pltpu.VMEM)
    return pl.pallas_call(
        factor_kernel,
        out_shape=[square] * 3,
        in_specs=[vmem] * 2,
        out_specs=[vmem] * 3,
        scratch_shapes=[pltpu.VMEM((order, 2 * order), jnp.float32)] * 2,
        name="factors",
    )(range_gram, corange_gram)


def body(snapshots, metrics, range_test, corange_test):
    space, win = lax.axis_size("space"), lax.axis_size("win")
    w = lax.axis_index("win")
    padded = padded_2(snapshots, (("space", 2),), 1)
    fields = derive(padded, metrics)
    tile_rows, columns = fields.shape[2], fields.shape[3]
    own = tile_rows // win
    sketch = jnp.einsum(
        "scxy,sk->xcky", fields, range_test, preferred_element_type=jnp.float32
    )
    total = lax.dynamic_slice_in_dim(sketch, w * own, own, 0)
    for d in range(1, win):
        ring = [(i, (i + d) % win) for i in range(win)]
        part = lax.dynamic_slice_in_dim(sketch, (w + d) % win * own, own, 0)
        part = lax.ppermute(part.astype(jnp.bfloat16), "win", ring)
        total = total + part.astype(jnp.float32)
    projection = jnp.einsum(
        "kcxy,scxy->sk", corange_test, fields, preferred_element_type=jnp.float32
    )
    snaps, rank = projection.shape
    shares = projection.reshape(space, snaps // space, rank)
    shares = lax.all_to_all(shares, "space", 0, 0, tiled=True)
    share = jnp.sum(shares, axis=0)
    corange_part = jnp.dot(share.T, share, precision=EXACT)
    range_part = jnp.einsum("xcky,xcjy->kj", total, total, precision=EXACT)
    grams = total_over_all(jnp.concatenate([range_part, corange_part], axis=1))
    cells = 3 * tile_rows * space * columns
    inverse, r_range, r_corange = factors(
        grams[:, :rank] / cells, grams[:, rank:] / (snaps * win)
    )
    q_basis = jnp.einsum("xcky,jk->xjcy", total, inverse, precision=EXACT)
    return (q_basis, r_range, r_corange)


def solution(mesh):
    placed = (
        P("win", None, "space", None),
        P(None, "space", None),
        P("win", None),
        P(None, None, "space", None),
    )
    return jax.shard_map(
        body,
        mesh=mesh,
        in_specs=placed,
        out_specs=(P(("space", "win"), None, None, None), P(), P()),
        check_vma=False,
    )
```

```python
import jax
import jax.numpy as jnp
from jax import lax
from jax.experimental import pallas as pl
from jax.experimental.pallas import tpu as pltpu
from jax.sharding import PartitionSpec as P

BOTH = ("space", "win")
EXACT = lax.Precision.HIGHEST


def hops(space, win):
    space_bits = [win << b for b in range(space.bit_length() - 1)]
    win_bits = [1 << b for b in range(win.bit_length() - 1)]
    stages = [space_bits[:1], win_bits[:1] + space_bits[1:2]]
    rest = win_bits[1:] + space_bits[2:]
    stages += [rest[i : i + 2] for i in range(0, len(rest), 2)]
    return [s for s in stages if s]


def total_over_all(value):
    space, win = lax.axis_size("space"), lax.axis_size("win")
    count = space * win
    if count & (count - 1) or win & (win - 1):
        return lax.psum(value, BOTH)
    for bits in hops(space, win):
        parts = {0: value}
        for b in bits:
            for mask in list(parts):
                pairs = [(i, i ^ mask ^ b) for i in range(count)]
                parts[mask ^ b] = lax.ppermute(value, BOTH, pairs)
        for b in bits:
            parts = {m: parts[m] + parts[m ^ b] for m in parts if not m & b}
        value = parts[0]
    return value


def eliminate(chains, step, save):
    order = chains[0].shape[0]
    for j in range(0, order, step):
        for m, matrix in enumerate(chains):
            cols = [jnp.broadcast_to(matrix[:, j + a : j + a + 1], matrix.shape) for a in range(step)]
            rows = [matrix[j + a : j + a + 1, :] for a in range(step)]
            top = j + step
            rest = matrix[top:, :]
            for a in range(step):
                pivot = cols[a][j + a : j + a + 1, :]
                scaled = rows[a] / pivot
                for c in range(a + 1, step):
                    ratio = cols[c][j + a : j + a + 1, :] / pivot
                    down = cols[a][j + c : j + c + 1, :]
                    cols[c] = cols[c] - cols[a] * ratio
                    rows[c] = rows[c] - scaled * down
                save(m, j + a, rows[a] * lax.rsqrt(pivot))
                if top < order:
                    rest = rest - cols[a][top:, :] * scaled
            if top < order:
                chains[m] = jnp.concatenate([matrix[:top, :], rest], axis=0)


NT = (((1,), (1,)), ((), ()))
TN = (((0,), (0,)), ((), ()))
F32, BF16 = jnp.float32, jnp.bfloat16


def vmem(count):
    return [pl.BlockSpec(memory_space=pltpu.VMEM)] * count


def small(limit):
    return pltpu.CompilerParams(vmem_limit_bytes=limit << 20)


def split(value):
    high = value.astype(BF16)
    return high, (value - high.astype(F32)).astype(BF16)


def front_kernel(win, at_ref, snaps_ref, low_ref, high_ref, metrics_ref, mix_ref, test_ref, own_ref, send_ref, proj_ref, wide_ref, sum_ref):
    tile, snaps, columns = snaps_ref.shape[1:]
    rank = mix_ref.shape[0]
    own = tile // win
    wide_ref[...] = test_ref[...].astype(F32).reshape(wide_ref.shape)
    sum_ref[...] = jnp.zeros_like(sum_ref)
    before = lax.broadcasted_iota(jnp.int32, (columns, columns), 0)
    after = lax.broadcasted_iota(jnp.int32, (columns, columns), 1)
    eta = ((before == after + 1).astype(F32) - (before == after - 1).astype(F32)).astype(BF16)
    mix = mix_ref[...]

    def row(x, lower, upper, store):
        def along(c):
            xi = upper(c).astype(F32) - lower(c).astype(F32)
            return xi, jnp.dot(snaps_ref[c, x], eta, preferred_element_type=F32)

        a, b, c, e = [metrics_ref[i, pl.ds(x, 1), :] * 0.5 for i in range(4)]
        (u_xi, u_eta), (v_xi, v_eta), (p_xi, p_eta) = along(0), along(1), along(2)
        vortex = a * v_xi + b * v_eta - c * u_xi - e * u_eta
        fields = [vortex, a * p_xi + b * p_eta, c * p_xi + e * p_eta]
        fields = jnp.concatenate([f.astype(BF16) for f in fields], axis=1)
        sketch = jnp.dot(mix, fields, preferred_element_type=F32)
        for i in range(3):
            store(i, sketch[:, i * columns : (i + 1) * columns])
        tests = [wide_ref[pl.ds(i * tile + x, rank, stride=3 * tile), :].astype(BF16) for i in range(3)]
        tests = jnp.concatenate(tests, axis=1)
        sum_ref[...] += lax.dot_general(fields, tests, NT, preferred_element_type=F32)

    for d in [*range(1, win), 0]:
        base = lax.rem(at_ref[0] + d, win) * own

        def store_at(r, d=d):
            def store(i, value):
                if d:
                    send_ref[d - 1, r, i] = value.astype(BF16)
                else:
                    own_ref[r, i] = value
            return store

        def inner(x):
            return lambda c: snaps_ref[c, x]

        def first(c, base=base):
            near = snaps_ref[c, jnp.maximum(base - 1, 0)]
            return jnp.where(base == 0, low_ref[c], near)

        def last(c, end=base + own):
            near = snaps_ref[c, jnp.minimum(end, tile - 1)]
            return jnp.where(end == tile, high_ref[c], near)

        def middle(r, carry, base=base, store_at=store_at):
            row(base + r, inner(base + r - 1), inner(base + r + 1), store_at(r))
            return carry

        if own == 1:
            row(base, first, last, store_at(0))
        else:
            row(base, first, inner(base + 1), store_at(0))
            lax.fori_loop(1, own - 1, middle, 0)
            row(base + own - 1, inner(base + own - 2), last, store_at(own - 1))
    half = snaps // 2
    proj_ref[...] = jnp.concatenate([sum_ref[:half, :], sum_ref[half:, :]], axis=1)


def front(at, snaps, low, high, metrics, mix, test, win):
    comps, tile, count, columns = snaps.shape
    rank = mix.shape[0]
    own = tile // win
    return pl.pallas_call(
        lambda *refs: front_kernel(win, *refs),
        out_shape=[
            jax.ShapeDtypeStruct((own, comps, rank, columns), F32),
            jax.ShapeDtypeStruct((win - 1, own, comps, rank, columns), BF16),
            jax.ShapeDtypeStruct((count // 2, 2 * rank), F32),
        ],
        in_specs=[pl.BlockSpec(memory_space=pltpu.SMEM), *vmem(6)],
        out_specs=vmem(3),
        scratch_shapes=[
            pltpu.VMEM((rank * comps * tile, columns), F32),
            pltpu.VMEM((count, rank), F32),
        ],
        compiler_params=small(20),
        name="front",
    )(at, snaps, low, high, metrics, mix, test)


def gram_kernel(own_ref, got_ref, shares_ref, stack_ref, gram_ref):
    own, comps, rank, columns = own_ref.shape
    for x in range(own):
        for c in range(comps):
            total = own_ref[x, c]
            for d in range(got_ref.shape[0]):
                total = total + got_ref[d, x, c].astype(F32)
            high, low = split(total)
            at = (x * comps + c) * columns
            stack_ref[:rank, at : at + columns] = high
            stack_ref[rank:, at : at + columns] = low
    stack = stack_ref[...]
    pair = lax.dot_general(stack, stack, NT, preferred_element_type=F32)
    gram = pair[:rank, :rank] + pair[:rank, rank:] + pair[rank:, :rank] + pair[rank:, rank:]
    share = shares_ref[0]
    for i in range(1, shares_ref.shape[0]):
        share = share + shares_ref[i]
    pair = lax.dot_general(share, share, TN, precision=EXACT, preferred_element_type=F32)
    gram_ref[:, :rank] = gram
    gram_ref[:, rank:] = pair[:rank, :rank] + pair[rank:, rank:]


def grams_of(own, got, shares):
    rows, comps, rank, columns = own.shape
    return pl.pallas_call(
        gram_kernel,
        out_shape=[
            jax.ShapeDtypeStruct((2 * rank, rows * comps * columns), BF16),
            jax.ShapeDtypeStruct((rank, 2 * rank), F32),
        ],
        in_specs=vmem(3),
        out_specs=vmem(2),
        compiler_params=small(16),
        name="grams",
    )(own, got, shares)


def finish_kernel(cells, snaps, gram_ref, stack_ref, q_ref, r_range_ref, r_corange_ref, wide_r, wide_c, out_ref, sems):
    rank = gram_ref.shape[0]
    row = lax.broadcasted_iota(jnp.int32, (rank, rank), 0)
    col = lax.broadcasted_iota(jnp.int32, (rank, rank), 1)
    eye = (row == col).astype(F32)
    held = (wide_r, wide_c)

    def save(m, r, value):
        held[m][r : r + 1, :] = value

    pair = (gram_ref[:, :rank] * (1.0 / cells), gram_ref[:, rank:] * (1.0 / snaps))
    chains = [jnp.concatenate([g, eye], axis=1) for g in pair]
    eliminate(chains, 8 if rank % 8 == 0 else 1, save)
    r_range_ref[...] = jnp.where(col >= row, wide_r[:, :rank], 0.0)
    r_corange_ref[...] = jnp.where(col >= row, wide_c[:, :rank], 0.0)
    high, low = split(jnp.where(col <= row, wide_r[:, rank:], 0.0))
    left = jnp.concatenate([high, high], axis=1)
    own, comps, _, columns = out_ref.shape
    width = comps * columns
    for x in range(own):
        right = stack_ref[:, x * width : (x + 1) * width]
        value = jnp.dot(left, right, preferred_element_type=F32)
        value = value + jnp.dot(low, right[:rank], preferred_element_type=F32)
        for c in range(comps):
            out_ref[x, c] = value[:, c * columns : (c + 1) * columns]
        pltpu.make_async_copy(out_ref.at[x], q_ref.at[x], sems.at[x]).start()
    for x in range(own):
        pltpu.make_async_copy(out_ref.at[x], q_ref.at[x], sems.at[x]).wait()


def finish(gram, stack, shape, cells, snaps):
    rank = gram.shape[0]
    square = jax.ShapeDtypeStruct((rank, rank), F32)
    return pl.pallas_call(
        lambda *refs: finish_kernel(cells, snaps, *refs),
        out_shape=[jax.ShapeDtypeStruct(shape, F32), square, square],
        in_specs=vmem(2),
        out_specs=[pl.BlockSpec(memory_space=pl.ANY), *vmem(2)],
        scratch_shapes=[
            *[pltpu.VMEM((rank, 2 * rank), F32)] * 2,
            pltpu.VMEM(shape, F32),
            pltpu.SemaphoreType.DMA((shape[0],)),
        ],
        compiler_params=small(16),
        name="finish",
    )(gram, stack)


def neighbours(value):
    count = lax.axis_size("space")
    up = [(i, i + 1) for i in range(count - 1)]
    down = [(j, i) for i, j in up]
    before = lax.ppermute(value[:, -1], "space", up)
    after = lax.ppermute(value[:, 0], "space", down)
    return before, after


def body(snapshots, metrics, range_test, corange_test):
    space, win = lax.axis_size("space"), lax.axis_size("win")
    w = lax.axis_index("win")
    snaps, comps, tile, columns = snapshots.shape
    rank = range_test.shape[1]
    turned = jnp.transpose(snapshots, (1, 2, 0, 3))
    before, after = neighbours(turned)
    own, send, projection = front(
        w.astype(jnp.int32).reshape(1), turned, before, after, metrics, range_test.T, corange_test, win
    )
    got = []
    for d in range(1, win):
        ring = [(i, (i + d) % win) for i in range(win)]
        got.append(lax.ppermute(send[d - 1], "win", ring))
    shares = projection.reshape(space, snaps // 2 // space, 2 * rank)
    shares = lax.all_to_all(shares, "space", 0, 0, tiled=True)
    stack, gram = grams_of(own, jnp.stack(got), shares)
    gram = total_over_all(gram)
    q_turned, r_range, r_corange = finish(
        gram, stack, own.shape, comps * tile * space * columns, snaps * win
    )
    return (jnp.transpose(q_turned, (0, 2, 1, 3)), r_range, r_corange)


def solution(mesh):
    placed = (
        P("win", None, "space", None),
        P(None, "space", None),
        P("win", None),
        P(None, None, "space", None),
    )
    return jax.shard_map(
        body,
        mesh=mesh,
        in_specs=placed,
        out_specs=(P(("space", "win"), None, None, None), P(), P()),
        check_vma=False,
    )
```

```python
import jax
import jax.numpy as jnp
from jax import lax
from jax.experimental import pallas as pl
from jax.experimental.pallas import tpu as pltpu
from jax.sharding import PartitionSpec as P

BOTH = ("space", "win")
EXACT = lax.Precision.HIGHEST


def hops(space, win):
    space_bits = [win << b for b in range(space.bit_length() - 1)]
    win_bits = [1 << b for b in range(win.bit_length() - 1)]
    stages = [space_bits[:1], win_bits[:1] + space_bits[1:2]]
    rest = win_bits[1:] + space_bits[2:]
    stages += [rest[i : i + 2] for i in range(0, len(rest), 2)]
    return [s for s in stages if s]


def total_over_all(value):
    space, win = lax.axis_size("space"), lax.axis_size("win")
    count = space * win
    if count & (count - 1) or win & (win - 1):
        return lax.psum(value, BOTH)
    for bits in hops(space, win):
        parts = {0: value}
        for b in bits:
            for mask in list(parts):
                pairs = [(i, i ^ mask ^ b) for i in range(count)]
                parts[mask ^ b] = lax.ppermute(value, BOTH, pairs)
        for b in bits:
            parts = {m: parts[m] + parts[m ^ b] for m in parts if not m & b}
        value = parts[0]
    return value


def eliminate(chains, step, save):
    order = chains[0].shape[0]
    for j in range(0, order, step):
        for m, matrix in enumerate(chains):
            cols = [jnp.broadcast_to(matrix[:, j + a : j + a + 1], matrix.shape) for a in range(step)]
            rows = [matrix[j + a : j + a + 1, :] for a in range(step)]
            top = j + step
            rest = matrix[top:, :]
            for a in range(step):
                pivot = cols[a][j + a : j + a + 1, :]
                scaled = rows[a] / pivot
                for c in range(a + 1, step):
                    ratio = cols[c][j + a : j + a + 1, :] / pivot
                    down = cols[a][j + c : j + c + 1, :]
                    cols[c] = cols[c] - cols[a] * ratio
                    rows[c] = rows[c] - scaled * down
                save(m, j + a, rows[a] * lax.rsqrt(pivot))
                if top < order:
                    rest = rest - cols[a][top:, :] * scaled
            if top < order:
                chains[m] = jnp.concatenate([matrix[:top, :], rest], axis=0)


NT = (((1,), (1,)), ((), ()))
TN = (((0,), (0,)), ((), ()))
F32, BF16 = jnp.float32, jnp.bfloat16


def vmem(count):
    return [pl.BlockSpec(memory_space=pltpu.VMEM)] * count


def small(limit):
    return pltpu.CompilerParams(vmem_limit_bytes=limit << 20)


def split(value):
    high = value.astype(BF16)
    return high, (value - high.astype(F32)).astype(BF16)


def edge_kernel(at_ref, turned_ref, edges_ref):
    tile = turned_ref.shape[1]
    odd = lax.rem(at_ref[1], 2)
    edges_ref[0] = turned_ref[:, odd * (tile - 1)]
    edges_ref[1] = turned_ref[:, (1 - odd) * (tile - 1)]


def edges_of(at, turned):
    comps, tile, snaps, columns = turned.shape
    return pl.pallas_call(
        edge_kernel,
        out_shape=jax.ShapeDtypeStruct((2, comps, snaps, columns), BF16),
        in_specs=[pl.BlockSpec(memory_space=pltpu.SMEM), *vmem(1)],
        out_specs=vmem(1)[0],
        compiler_params=small(8),
        name="edges",
    )(at, turned)


def eta_matrix(columns):
    before = lax.broadcasted_iota(jnp.int32, (columns, columns), 0)
    after = lax.broadcasted_iota(jnp.int32, (columns, columns), 1)
    return ((before == after + 1).astype(F32) - (before == after - 1).astype(F32)).astype(BF16)


def field_rows(metrics_ref, x, xi, eta):
    a, b, c, e = [metrics_ref[i, x : x + 1, :] * 0.5 for i in range(4)]
    vortex = a * xi[1] + b * eta[1] - c * xi[0] - e * eta[0]
    rows = [vortex, a * xi[2] + b * eta[2], c * xi[2] + e * eta[2]]
    return [row.astype(BF16) for row in rows]


def inner_kernel(turned_ref, metrics_ref, fields_ref, eta_ref):
    comps, tile, snaps, columns = turned_ref.shape
    half = snaps // 2
    one = eta_matrix(columns)
    none = jnp.zeros_like(one)
    pair = jnp.concatenate(
        [jnp.concatenate([one, none], axis=1), jnp.concatenate([none, one], axis=1)], axis=0
    )
    here = jnp.concatenate([turned_ref[:, :, :half, :], turned_ref[:, :, half:, :]], axis=3)
    here = here.reshape(comps * tile * half, 2 * columns)
    eta_ref[...] = jnp.dot(here, pair, preferred_element_type=F32)
    part = min(half, 32)
    for s in range(0, snaps, part):
        lane = s // half * columns

        def layer(x):
            return [turned_ref[c, x, s : s + part, :].astype(F32) for c in range(comps)]

        below, level = layer(0), layer(1)
        for x in range(1, tile - 1):
            above = layer(x + 1)
            xi = [up - down for up, down in zip(above, below)]
            at = [(c * tile + x) * half + s % half for c in range(comps)]
            eta = [eta_ref[i : i + part, lane : lane + columns] for i in at]
            for i, row in enumerate(field_rows(metrics_ref, x, xi, eta)):
                fields_ref[x, s : s + part, i * columns : (i + 1) * columns] = row
            below, level = level, above


def inner_fields(turned, metrics):
    comps, tile, snaps, columns = turned.shape
    return pl.pallas_call(
        inner_kernel,
        out_shape=jax.ShapeDtypeStruct((tile, snaps, comps * columns), BF16),
        in_specs=vmem(2),
        out_specs=vmem(1)[0],
        scratch_shapes=[pltpu.VMEM((comps * tile * snaps // 2, 2 * columns), F32)],
        compiler_params=small(14),
        cost_estimate=pl.CostEstimate(flops=10**9, bytes_accessed=4 * 10**6, transcendentals=0),
        name="inner",
    )(turned, metrics)


def sketch_kernel(win, at_ref, turned_ref, fields_ref, far_ref, near_ref, metrics_ref, mix_ref, own_ref, send_ref, edge_ref):
    comps, tile, snaps, columns = turned_ref.shape
    own = tile // win
    odd = lax.rem(at_ref[1], 2) == 1
    one = eta_matrix(columns)
    for side, x in ((0, 0), (1, tile - 1)):
        xi, eta = [], []
        for c in range(comps):
            far, near = far_ref[c].astype(F32), near_ref[c].astype(F32)
            if side:
                upper, lower = jnp.where(odd, far, near), turned_ref[c, x - 1].astype(F32)
            else:
                upper, lower = turned_ref[c, x + 1].astype(F32), jnp.where(odd, near, far)
            xi.append(upper - lower)
            eta.append(jnp.dot(turned_ref[c, x], one, preferred_element_type=F32))
        for i, row in enumerate(field_rows(metrics_ref, x, xi, eta)):
            edge_ref[side, :, i * columns : (i + 1) * columns] = row
    mix = mix_ref[...]
    for d in [*range(1, win), 0]:
        base = lax.rem(at_ref[0] + d, win) * own
        for r in range(own):
            layer = fields_ref[base + r]
            if r == 0:
                layer = jnp.where(base == 0, edge_ref[0], layer)
            if r == own - 1:
                layer = jnp.where(base + own == tile, edge_ref[1], layer)
            sketch = jnp.dot(mix, layer, preferred_element_type=F32)
            for i in range(comps):
                value = sketch[:, i * columns : (i + 1) * columns]
                if d:
                    send_ref[d - 1, r, i] = value.astype(BF16)
                else:
                    own_ref[r, i] = value


def sketch_of(at, turned, fields, far, near, metrics, mix, win):
    comps, tile, snaps, columns = turned.shape
    rank = mix.shape[0]
    own = tile // win
    return pl.pallas_call(
        lambda *refs: sketch_kernel(win, *refs),
        out_shape=[
            jax.ShapeDtypeStruct((own, comps, rank, columns), F32),
            jax.ShapeDtypeStruct((win - 1, own, comps, rank, columns), BF16),
            jax.ShapeDtypeStruct((2, snaps, comps * columns), BF16),
        ],
        in_specs=[pl.BlockSpec(memory_space=pltpu.SMEM), *vmem(6)],
        out_specs=vmem(3),
        compiler_params=small(14),
        name="sketch",
    )(at, turned, fields, far, near, metrics, mix)


def project_kernel(fields_ref, edge_ref, tests_ref, proj_ref):
    comps, tile, _, _ = tests_ref.shape
    snaps = fields_ref.shape[1]
    inner = [fields_ref[x] for x in range(1, tile - 1)]
    fields = jnp.concatenate([edge_ref[0], *inner, edge_ref[1]], axis=1)
    tests = jnp.concatenate([tests_ref[c, x] for x in range(tile) for c in range(comps)], axis=1)
    total = lax.dot_general(fields, tests, NT, preferred_element_type=F32)
    half = snaps // 2
    proj_ref[...] = jnp.concatenate([total[:half, :], total[half:, :]], axis=1)


def project(fields, edges, tests):
    snaps, rank = fields.shape[1], tests.shape[2]
    return pl.pallas_call(
        project_kernel,
        out_shape=jax.ShapeDtypeStruct((snaps // 2, 2 * rank), F32),
        in_specs=vmem(3),
        out_specs=vmem(1)[0],
        compiler_params=small(14),
        name="project",
    )(fields, edges, tests)


def gram_kernel(own_ref, got_ref, shares_ref, stack_ref, gram_ref):
    own, comps, rank, columns = own_ref.shape
    for x in range(own):
        for c in range(comps):
            total = own_ref[x, c]
            for d in range(got_ref.shape[0]):
                total = total + got_ref[d, x, c].astype(F32)
            high, low = split(total)
            at = (x * comps + c) * columns
            stack_ref[:rank, at : at + columns] = high
            stack_ref[rank:, at : at + columns] = low
    stack = stack_ref[...]
    pair = lax.dot_general(stack, stack, NT, preferred_element_type=F32)
    gram = pair[:rank, :rank] + pair[:rank, rank:] + pair[rank:, :rank] + pair[rank:, rank:]
    share = shares_ref[0]
    for i in range(1, shares_ref.shape[0]):
        share = share + shares_ref[i]
    pair = lax.dot_general(share, share, TN, precision=EXACT, preferred_element_type=F32)
    other = pair[:rank, :rank] + pair[rank:, rank:]
    row = lax.broadcasted_iota(jnp.int32, (rank, rank), 0)
    col = lax.broadcasted_iota(jnp.int32, (rank, rank), 1)
    both = jnp.where(col >= row, gram, other)
    half = rank // 2
    gram_ref[:half, :rank] = both[:half]
    gram_ref[:half, rank:] = both[half:]
    gram_ref[half:, :] = jnp.zeros_like(gram_ref[half:, :])
    gram_ref[half : half + 1, :rank] = jnp.sum(jnp.where(col == row, other, 0.0), axis=0, keepdims=True)


def grams_of(own, got, shares):
    rows, comps, rank, columns = own.shape
    return pl.pallas_call(
        gram_kernel,
        out_shape=[
            jax.ShapeDtypeStruct((2 * rank, rows * comps * columns), BF16),
            jax.ShapeDtypeStruct((rank // 2 + 8, 2 * rank), F32),
        ],
        in_specs=vmem(3),
        out_specs=vmem(2),
        compiler_params=small(16),
        name="grams",
    )(own, got, shares)


def finish_kernel(cells, snaps, gram_ref, stack_ref, q_ref, r_range_ref, r_corange_ref, wide_r, wide_c, out_ref, sems):
    rank = r_range_ref.shape[0]
    row = lax.broadcasted_iota(jnp.int32, (rank, rank), 0)
    col = lax.broadcasted_iota(jnp.int32, (rank, rank), 1)
    eye = (row == col).astype(F32)
    held = (wide_r, wide_c)

    def save(m, r, value):
        held[m][r : r + 1, :] = value

    half = rank // 2
    both = jnp.concatenate([gram_ref[:half, :rank], gram_ref[:half, rank:]], axis=0)
    turned = both.T
    diagonal = gram_ref[half : half + 1, :rank]
    gram = jnp.where(col >= row, both, turned)
    other = jnp.where(col == row, diagonal, jnp.where(col > row, turned, both))
    pair = (gram / cells, other / snaps)
    chains = [jnp.concatenate([g, eye], axis=1) for g in pair]
    eliminate(chains, 8 if rank % 8 == 0 else 1, save)
    r_range_ref[...] = jnp.where(col >= row, wide_r[:, :rank], 0.0)
    r_corange_ref[...] = jnp.where(col >= row, wide_c[:, :rank], 0.0)
    high, low = split(jnp.where(col <= row, wide_r[:, rank:], 0.0))
    left = jnp.concatenate([high, high], axis=1)
    own, comps, _, columns = out_ref.shape
    width = comps * columns
    for x in range(own):
        right = stack_ref[:, x * width : (x + 1) * width]
        value = jnp.dot(left, right, preferred_element_type=F32)
        value = value + jnp.dot(low, right[:rank], preferred_element_type=F32)
        for c in range(comps):
            out_ref[x, c] = value[:, c * columns : (c + 1) * columns]
        pltpu.make_async_copy(out_ref.at[x], q_ref.at[x], sems.at[x]).start()
    for x in range(own):
        pltpu.make_async_copy(out_ref.at[x], q_ref.at[x], sems.at[x]).wait()


def finish(gram, stack, shape, cells, snaps):
    rank = shape[2]
    square = jax.ShapeDtypeStruct((rank, rank), F32)
    return pl.pallas_call(
        lambda *refs: finish_kernel(cells, snaps, *refs),
        out_shape=[jax.ShapeDtypeStruct(shape, F32), square, square],
        in_specs=vmem(2),
        out_specs=[pl.BlockSpec(memory_space=pl.ANY), *vmem(2)],
        scratch_shapes=[
            *[pltpu.VMEM((rank, 2 * rank), F32)] * 2,
            pltpu.VMEM(shape, F32),
            pltpu.SemaphoreType.DMA((shape[0],)),
        ],
        compiler_params=small(16),
        name="finish",
    )(gram, stack)


def swapped(edges):
    count = lax.axis_size("space")
    across = [(i, i + 1) for i in range(1, count - 1, 2)]
    within = [(i, i + 1) for i in range(0, count - 1, 2)]
    far = lax.ppermute(edges[0], "space", across + [(j, i) for i, j in across])
    near = lax.ppermute(edges[1], "space", within + [(j, i) for i, j in within])
    return far, near


def body(snapshots, metrics, range_test, corange_test):
    space, win = lax.axis_size("space"), lax.axis_size("win")
    snaps, comps, tile, columns = snapshots.shape
    rank = range_test.shape[1]
    at = jnp.stack([lax.axis_index("win"), lax.axis_index("space")]).astype(jnp.int32)
    turned = jnp.transpose(snapshots, (1, 2, 0, 3))
    far, near = swapped(edges_of(at, turned))
    fields = inner_fields(turned, metrics)
    own, send, edges = sketch_of(at, turned, fields, far, near, metrics, range_test.T, win)
    got = []
    for d in range(1, win):
        ring = [(i, (i + d) % win) for i in range(win)]
        got.append(lax.ppermute(send[d - 1], "win", ring))
    projection = project(fields, edges, jnp.transpose(corange_test, (1, 2, 0, 3)))
    shares = projection.reshape(space, snaps // 2 // space, 2 * rank)
    shares = lax.all_to_all(shares, "space", 0, 0, tiled=True)
    stack, gram = grams_of(own, jnp.stack(got), shares)
    gram = total_over_all(gram)
    q_turned, r_range, r_corange = finish(
        gram, stack, own.shape, comps * tile * space * columns, snaps * win
    )
    return (jnp.transpose(q_turned, (0, 2, 1, 3)), r_range, r_corange)


def solution(mesh):
    placed = (
        P("win", None, "space", None),
        P(None, "space", None),
        P("win", None),
        P(None, None, "space", None),
    )
    return jax.shard_map(
        body,
        mesh=mesh,
        in_specs=placed,
        out_specs=(P(("space", "win"), None, None, None), P(), P()),
        check_vma=False,
    )
```

```python
import jax
import jax.numpy as jnp
from jax import lax
from jax.experimental import pallas as pl
from jax.experimental.pallas import tpu as pltpu
from jax.sharding import PartitionSpec as P

BOTH = ("space", "win")
EXACT = lax.Precision.HIGHEST


def hops(space, win):
    space_bits = [win << b for b in range(space.bit_length() - 1)]
    win_bits = [1 << b for b in range(win.bit_length() - 1)]
    stages = [space_bits[:1], win_bits[:1] + space_bits[1:2]]
    rest = win_bits[1:] + space_bits[2:]
    stages += [rest[i : i + 2] for i in range(0, len(rest), 2)]
    return [s for s in stages if s]


def total_over_all(value):
    space, win = lax.axis_size("space"), lax.axis_size("win")
    count = space * win
    if count & (count - 1) or win & (win - 1):
        return lax.psum(value, BOTH)
    for bits in hops(space, win):
        parts = {0: value}
        for b in bits:
            for mask in list(parts):
                pairs = [(i, i ^ mask ^ b) for i in range(count)]
                parts[mask ^ b] = lax.ppermute(value, BOTH, pairs)
        for b in bits:
            parts = {m: parts[m] + parts[m ^ b] for m in parts if not m & b}
        value = parts[0]
    return value


def eliminate(chains, step, save):
    order = chains[0].shape[0]
    for j in range(0, order, step):
        for m, rest in enumerate(chains):
            cols = [jnp.broadcast_to(rest[:, j + a : j + a + 1], rest.shape) for a in range(step)]
            rows = [rest[a : a + 1, :] for a in range(step)]
            rest = rest[step:, :]
            for a in range(step):
                pivot = cols[a][a : a + 1, :]
                scaled = rows[a] / pivot
                for c in range(a + 1, step):
                    ratio = cols[c][a : a + 1, :] / pivot
                    down = cols[a][c : c + 1, :]
                    cols[c] = cols[c] - cols[a] * ratio
                    rows[c] = rows[c] - scaled * down
                save(m, j + a, rows[a] * lax.rsqrt(pivot))
                if j + step < order:
                    rest = rest - cols[a][step:, :] * scaled
            chains[m] = rest


NT = (((1,), (1,)), ((), ()))
TN = (((0,), (0,)), ((), ()))
F32, BF16 = jnp.float32, jnp.bfloat16


def vmem(count):
    return [pl.BlockSpec(memory_space=pltpu.VMEM)] * count


def small(limit):
    return pltpu.CompilerParams(vmem_limit_bytes=limit << 20)


def split(value):
    high = value.astype(BF16)
    return high, (value - high.astype(F32)).astype(BF16)


def edge_kernel(turned_ref, edges_ref):
    tile = turned_ref.shape[1]
    odd = lax.rem(lax.axis_index("space"), 2)
    edges_ref[0] = turned_ref[:, odd * (tile - 1)]
    edges_ref[1] = turned_ref[:, (1 - odd) * (tile - 1)]


def edges_of(turned):
    comps, tile, snaps, columns = turned.shape
    return pl.pallas_call(
        edge_kernel,
        out_shape=jax.ShapeDtypeStruct((2, comps, snaps, columns), BF16),
        in_specs=vmem(1),
        out_specs=vmem(1)[0],
        compiler_params=small(8),
        name="edges",
    )(turned)


def eta_matrix(columns):
    before = lax.broadcasted_iota(jnp.int32, (columns, columns), 0)
    after = lax.broadcasted_iota(jnp.int32, (columns, columns), 1)
    return ((before == after + 1).astype(F32) - (before == after - 1).astype(F32)).astype(BF16)


def field_rows(metrics_ref, x, xi, eta):
    a, b, c, e = [metrics_ref[i, x : x + 1, :] * 0.5 for i in range(4)]
    vortex = a * xi[1] + b * eta[1] - c * xi[0] - e * eta[0]
    rows = [vortex, a * xi[2] + b * eta[2], c * xi[2] + e * eta[2]]
    return [row.astype(BF16) for row in rows]


def inner_kernel(turned_ref, metrics_ref, fields_ref, eta_ref):
    comps, tile, snaps, columns = turned_ref.shape
    half = snaps // 2
    one = eta_matrix(columns)
    none = jnp.zeros_like(one)
    pair = jnp.concatenate(
        [jnp.concatenate([one, none], axis=1), jnp.concatenate([none, one], axis=1)], axis=0
    )
    here = jnp.concatenate([turned_ref[:, :, :half, :], turned_ref[:, :, half:, :]], axis=3)
    here = here.reshape(comps * tile * half, 2 * columns)
    eta_ref[...] = jnp.dot(here, pair, preferred_element_type=F32)
    part = min(half, 32)
    for s in range(0, snaps, part):
        lane = s // half * columns

        def layer(x):
            return [turned_ref[c, x, s : s + part, :].astype(F32) for c in range(comps)]

        below, level = layer(0), layer(1)
        for x in range(1, tile - 1):
            above = layer(x + 1)
            xi = [up - down for up, down in zip(above, below)]
            at = [(c * tile + x) * half + s % half for c in range(comps)]
            eta = [eta_ref[i : i + part, lane : lane + columns] for i in at]
            for i, row in enumerate(field_rows(metrics_ref, x, xi, eta)):
                fields_ref[x, s : s + part, i * columns : (i + 1) * columns] = row
            below, level = level, above


def inner_fields(turned, metrics):
    comps, tile, snaps, columns = turned.shape
    return pl.pallas_call(
        inner_kernel,
        out_shape=jax.ShapeDtypeStruct((tile, snaps, comps * columns), BF16),
        in_specs=vmem(2),
        out_specs=vmem(1)[0],
        scratch_shapes=[pltpu.VMEM((comps * tile * snaps // 2, 2 * columns), F32)],
        compiler_params=small(14),
        cost_estimate=pl.CostEstimate(flops=10**9, bytes_accessed=4 * 10**6, transcendentals=0),
        name="inner",
    )(turned, metrics)


def sketch_rows(win, d, fields_ref, edge_ref, mix_ref, store):
    tile, _, width = fields_ref.shape
    own, columns = tile // win, width // 3
    base = lax.rem(lax.axis_index("win") + d, win) * own
    for r in range(own):
        layer = fields_ref[base + r]
        if r == 0:
            layer = jnp.where(base == 0, edge_ref[0], layer)
        if r == own - 1:
            layer = jnp.where(base + own == tile, edge_ref[1], layer)
        sketch = jnp.dot(mix_ref[...], layer, preferred_element_type=F32)
        for i in range(3):
            store(r, i, sketch[:, i * columns : (i + 1) * columns])


def sketch_kernel(win, turned_ref, fields_ref, far_ref, near_ref, metrics_ref, mix_ref, send_ref, edge_ref):
    comps, tile, snaps, columns = turned_ref.shape
    odd = lax.rem(lax.axis_index("space"), 2) == 1
    one = eta_matrix(columns)
    for side, x in ((0, 0), (1, tile - 1)):
        xi, eta = [], []
        for c in range(comps):
            far, near = far_ref[c].astype(F32), near_ref[c].astype(F32)
            if side:
                upper, lower = jnp.where(odd, far, near), turned_ref[c, x - 1].astype(F32)
            else:
                upper, lower = turned_ref[c, x + 1].astype(F32), jnp.where(odd, near, far)
            xi.append(upper - lower)
            eta.append(jnp.dot(turned_ref[c, x], one, preferred_element_type=F32))
        for i, row in enumerate(field_rows(metrics_ref, x, xi, eta)):
            edge_ref[side, :, i * columns : (i + 1) * columns] = row
    for d in range(1, win):
        sketch_rows(win, d, fields_ref, edge_ref, mix_ref, lambda r, i, v, d=d: send_ref.__setitem__((d - 1, r, i), v.astype(BF16)))


def sketch_of(turned, fields, far, near, metrics, mix, win):
    comps, tile, snaps, columns = turned.shape
    rank = mix.shape[0]
    own = tile // win
    return pl.pallas_call(
        lambda *refs: sketch_kernel(win, *refs),
        out_shape=[
            jax.ShapeDtypeStruct((win - 1, own, comps, rank, columns), BF16),
            jax.ShapeDtypeStruct((2, snaps, comps * columns), BF16),
        ],
        in_specs=vmem(6),
        out_specs=vmem(2),
        compiler_params=small(14),
        name="sketch",
    )(turned, fields, far, near, metrics, mix)


def project_kernel(win, fields_ref, edge_ref, tests_ref, mix_ref, proj_ref, own_ref):
    comps, tile, _, _ = tests_ref.shape
    snaps = fields_ref.shape[1]
    inner = [fields_ref[x] for x in range(1, tile - 1)]
    fields = jnp.concatenate([edge_ref[0], *inner, edge_ref[1]], axis=1)
    tests = jnp.concatenate([tests_ref[c, x] for x in range(tile) for c in range(comps)], axis=1)
    total = lax.dot_general(fields, tests, NT, preferred_element_type=F32)
    half = snaps // 2
    proj_ref[...] = jnp.concatenate([total[:half, :], total[half:, :]], axis=1)
    sketch_rows(win, 0, fields_ref, edge_ref, mix_ref, lambda r, i, v: own_ref.__setitem__((r, i), v))


def project(fields, edges, tests, mix, win):
    tile, snaps, width = fields.shape
    comps, _, rank, columns = tests.shape
    return pl.pallas_call(
        lambda *refs: project_kernel(win, *refs),
        out_shape=[
            jax.ShapeDtypeStruct((snaps // 2, 2 * rank), F32),
            jax.ShapeDtypeStruct((tile // win, comps, rank, columns), F32),
        ],
        in_specs=vmem(4),
        out_specs=vmem(2),
        compiler_params=small(14),
        name="project",
    )(fields, edges, tests, mix)


def gram_kernel(own_ref, got_ref, shares_ref, stack_ref, gram_ref):
    own, comps, rank, columns = own_ref.shape
    for x in range(own):
        for c in range(comps):
            total = own_ref[x, c]
            for d in range(got_ref.shape[0]):
                total = total + got_ref[d, x, c].astype(F32)
            high, low = split(total)
            at = (x * comps + c) * columns
            stack_ref[:rank, at : at + columns] = high
            stack_ref[rank : 2 * rank, at : at + columns] = low
            stack_ref[2 * rank :, at : at + columns] = high
    stack = stack_ref[: 2 * rank, :]
    pair = lax.dot_general(stack, stack, NT, preferred_element_type=F32)
    gram = pair[:rank, :rank] + pair[:rank, rank:] + pair[rank:, :rank] + pair[rank:, rank:]
    share = shares_ref[0]
    for i in range(1, shares_ref.shape[0]):
        share = share + shares_ref[i]
    pair = lax.dot_general(share, share, TN, precision=EXACT, preferred_element_type=F32)
    other = pair[:rank, :rank] + pair[rank:, rank:]
    row = lax.broadcasted_iota(jnp.int32, (rank, rank), 0)
    col = lax.broadcasted_iota(jnp.int32, (rank, rank), 1)
    both = jnp.where(col >= row, gram, other)
    half = rank // 2
    gram_ref[:half, :rank] = both[:half]
    gram_ref[:half, rank:] = both[half:]
    gram_ref[half:, :] = jnp.zeros_like(gram_ref[half:, :])
    gram_ref[half : half + 1, :rank] = jnp.sum(jnp.where(col == row, other, 0.0), axis=0, keepdims=True)


def grams_of(own, got, shares):
    rows, comps, rank, columns = own.shape
    return pl.pallas_call(
        gram_kernel,
        out_shape=[
            jax.ShapeDtypeStruct((3 * rank, rows * comps * columns), BF16),
            jax.ShapeDtypeStruct((rank // 2 + 8, 2 * rank), F32),
        ],
        in_specs=vmem(3),
        out_specs=vmem(2),
        compiler_params=small(16),
        name="grams",
    )(own, got, shares)


def finish_kernel(cells, snaps, gram_ref, stack_ref, q_ref, r_range_ref, r_corange_ref, wide_r, wide_c, out_ref, sems):
    rank = r_range_ref.shape[0]
    row = lax.broadcasted_iota(jnp.int32, (rank, rank), 0)
    col = lax.broadcasted_iota(jnp.int32, (rank, rank), 1)
    eye = (row == col).astype(F32)
    held = (wide_r, wide_c)

    def save(m, r, value):
        held[m][r : r + 1, :] = value

    half = rank // 2
    both = jnp.concatenate([gram_ref[:half, :rank], gram_ref[:half, rank:]], axis=0)
    turned = both.T
    diagonal = gram_ref[half : half + 1, :rank]
    gram = jnp.where(col >= row, both, turned)
    other = jnp.where(col == row, diagonal, jnp.where(col > row, turned, both))
    pair = (gram / cells, other / snaps)
    chains = [jnp.concatenate([g, eye], axis=1) for g in pair]
    eliminate(chains, 8 if rank % 8 == 0 else 1, save)
    r_range_ref[...] = jnp.where(col >= row, wide_r[:, :rank], 0.0)
    r_corange_ref[...] = jnp.where(col >= row, wide_c[:, :rank], 0.0)
    high, low = split(jnp.where(col <= row, wide_r[:, rank:], 0.0))
    left = jnp.concatenate([high, high, low], axis=1)
    own, comps, _, columns = out_ref.shape
    width = comps * columns
    for x in range(own):
        right = stack_ref[:, x * width : (x + 1) * width]
        value = jnp.dot(left, right, preferred_element_type=F32)
        for c in range(comps):
            out_ref[x, c] = value[:, c * columns : (c + 1) * columns]
        pltpu.make_async_copy(out_ref.at[x], q_ref.at[x], sems.at[x]).start()
    for x in range(own):
        pltpu.make_async_copy(out_ref.at[x], q_ref.at[x], sems.at[x]).wait()


def finish(gram, stack, shape, cells, snaps):
    rank = shape[2]
    square = jax.ShapeDtypeStruct((rank, rank), F32)
    return pl.pallas_call(
        lambda *refs: finish_kernel(cells, snaps, *refs),
        out_shape=[jax.ShapeDtypeStruct(shape, F32), square, square],
        in_specs=vmem(2),
        out_specs=[pl.BlockSpec(memory_space=pl.ANY), *vmem(2)],
        scratch_shapes=[
            *[pltpu.VMEM((rank, 2 * rank), F32)] * 2,
            pltpu.VMEM(shape, F32),
            pltpu.SemaphoreType.DMA((shape[0],)),
        ],
        compiler_params=small(16),
        name="finish",
    )(gram, stack)


def swapped(edges):
    count = lax.axis_size("space")
    across = [(i, i + 1) for i in range(1, count - 1, 2)]
    within = [(i, i + 1) for i in range(0, count - 1, 2)]
    far = lax.ppermute(edges[0], "space", across + [(j, i) for i, j in across])
    near = lax.ppermute(edges[1], "space", within + [(j, i) for i, j in within])
    return far, near


def body(snapshots, metrics, range_test, corange_test):
    space, win = lax.axis_size("space"), lax.axis_size("win")
    snaps, comps, tile, columns = snapshots.shape
    rank = range_test.shape[1]
    turned = jnp.transpose(snapshots, (1, 2, 0, 3))
    far, near = swapped(edges_of(turned))
    fields = inner_fields(turned, metrics)
    send, edges = sketch_of(turned, fields, far, near, metrics, range_test.T, win)
    got = []
    for d in range(1, win):
        ring = [(i, (i + d) % win) for i in range(win)]
        got.append(lax.ppermute(send[d - 1], "win", ring))
    projection, own = project(fields, edges, jnp.transpose(corange_test, (1, 2, 0, 3)), range_test.T, win)
    shares = projection.reshape(space, snaps // 2 // space, 2 * rank)
    shares = lax.all_to_all(shares, "space", 0, 0, tiled=True)
    stack, gram = grams_of(own, jnp.stack(got), shares)
    gram = total_over_all(gram)
    q_turned, r_range, r_corange = finish(
        gram, stack, own.shape, comps * tile * space * columns, snaps * win
    )
    return (jnp.transpose(q_turned, (0, 2, 1, 3)), r_range, r_corange)


def solution(mesh):
    placed = (
        P("win", None, "space", None),
        P(None, "space", None),
        P("win", None),
        P(None, None, "space", None),
    )
    return jax.shard_map(
        body,
        mesh=mesh,
        in_specs=placed,
        out_specs=(P(("space", "win"), None, None, None), P(), P()),
        check_vma=False,
    )
```

```python
import jax
import jax.numpy as jnp
from jax import lax
from jax.experimental import pallas as pl
from jax.experimental.pallas import tpu as pltpu
from jax.sharding import PartitionSpec as P

BOTH = ("space", "win")
EXACT = lax.Precision.HIGHEST


def hops(space, win):
    space_bits = [win << b for b in range(space.bit_length() - 1)]
    win_bits = [1 << b for b in range(win.bit_length() - 1)]
    stages = [space_bits[:1], win_bits[:1] + space_bits[1:2]]
    rest = win_bits[1:] + space_bits[2:]
    stages += [rest[i : i + 2] for i in range(0, len(rest), 2)]
    return [s for s in stages if s]


def total_over_all(value):
    space, win = lax.axis_size("space"), lax.axis_size("win")
    count = space * win
    if count & (count - 1) or win & (win - 1):
        return lax.psum(value, BOTH)
    for bits in hops(space, win):
        parts = {0: value}
        for b in bits:
            for mask in list(parts):
                pairs = [(i, i ^ mask ^ b) for i in range(count)]
                parts[mask ^ b] = lax.ppermute(value, BOTH, pairs)
        for b in bits:
            parts = {m: parts[m] + parts[m ^ b] for m in parts if not m & b}
        value = parts[0]
    return value


def eliminate(chains, step, save):
    order = chains[0].shape[0]
    for j in range(0, order, step):
        for m, rest in enumerate(chains):
            cols = [jnp.broadcast_to(rest[:, j + a : j + a + 1], rest.shape) for a in range(step)]
            rows = [rest[a : a + 1, :] for a in range(step)]
            rest = rest[step:, :]
            for a in range(step):
                pivot = cols[a][a : a + 1, :]
                scaled = rows[a] / pivot
                for c in range(a + 1, step):
                    ratio = cols[c][a : a + 1, :] / pivot
                    down = cols[a][c : c + 1, :]
                    cols[c] = cols[c] - cols[a] * ratio
                    rows[c] = rows[c] - scaled * down
                save(m, j + a, rows[a] * lax.rsqrt(pivot))
                if j + step < order:
                    rest = rest - cols[a][step:, :] * scaled
            chains[m] = rest


NT = (((1,), (1,)), ((), ()))
TN = (((0,), (0,)), ((), ()))
F32, BF16 = jnp.float32, jnp.bfloat16


def vmem(count):
    return [pl.BlockSpec(memory_space=pltpu.VMEM)] * count


def small(limit):
    return pltpu.CompilerParams(vmem_limit_bytes=limit << 20)


def split(value):
    high = value.astype(BF16)
    return high, (value - high.astype(F32)).astype(BF16)


def edge_kernel(turned_ref, edges_ref):
    tile = turned_ref.shape[1]
    odd = lax.rem(lax.axis_index("space"), 2)
    edges_ref[0] = turned_ref[:, odd * (tile - 1)]
    edges_ref[1] = turned_ref[:, (1 - odd) * (tile - 1)]


def edges_of(turned):
    comps, tile, snaps, columns = turned.shape
    return pl.pallas_call(
        edge_kernel,
        out_shape=jax.ShapeDtypeStruct((2, comps, snaps, columns), BF16),
        in_specs=vmem(1),
        out_specs=vmem(1)[0],
        compiler_params=small(8),
        name="edges",
    )(turned)


def eta_matrix(columns):
    before = lax.broadcasted_iota(jnp.int32, (columns, columns), 0)
    after = lax.broadcasted_iota(jnp.int32, (columns, columns), 1)
    return ((before == after + 1).astype(F32) - (before == after - 1).astype(F32)).astype(BF16)


def field_rows(metrics_ref, x, xi, eta):
    a, b, c, e = [metrics_ref[i, x : x + 1, :] * 0.5 for i in range(4)]
    vortex = a * xi[1] + b * eta[1] - c * xi[0] - e * eta[0]
    rows = [vortex, a * xi[2] + b * eta[2], c * xi[2] + e * eta[2]]
    return [row.astype(BF16) for row in rows]


def inner_kernel(turned_ref, metrics_ref, fields_ref, eta_ref):
    comps, tile, snaps, columns = turned_ref.shape
    half = snaps // 2
    one = eta_matrix(columns)
    none = jnp.zeros_like(one)
    pair = jnp.concatenate(
        [jnp.concatenate([one, none], axis=1), jnp.concatenate([none, one], axis=1)], axis=0
    )
    here = jnp.concatenate([turned_ref[:, :, :half, :], turned_ref[:, :, half:, :]], axis=3)
    here = here.reshape(comps * tile * half, 2 * columns)
    eta_ref[...] = jnp.dot(here, pair, preferred_element_type=F32)
    part = min(half, 32)
    for s in range(0, snaps, part):
        lane = s // half * columns

        def layer(x):
            return [turned_ref[c, x, s : s + part, :].astype(F32) for c in range(comps)]

        below, level = layer(0), layer(1)
        for x in range(1, tile - 1):
            above = layer(x + 1)
            xi = [up - down for up, down in zip(above, below)]
            at = [(c * tile + x) * half + s % half for c in range(comps)]
            eta = [eta_ref[i : i + part, lane : lane + columns] for i in at]
            for i, row in enumerate(field_rows(metrics_ref, x, xi, eta)):
                fields_ref[x, s : s + part, i * columns : (i + 1) * columns] = row
            below, level = level, above


def inner_fields(turned, metrics):
    comps, tile, snaps, columns = turned.shape
    return pl.pallas_call(
        inner_kernel,
        out_shape=jax.ShapeDtypeStruct((tile, snaps, comps * columns), BF16),
        in_specs=vmem(2),
        out_specs=vmem(1)[0],
        scratch_shapes=[pltpu.VMEM((comps * tile * snaps // 2, 2 * columns), F32)],
        compiler_params=small(14),
        cost_estimate=pl.CostEstimate(flops=10**9, bytes_accessed=4 * 10**6, transcendentals=0),
        name="inner",
    )(turned, metrics)


def chunks(window, own):
    half = own // 2
    return (jnp.where(window == 0, own - half, 0), half), (jnp.where(window == 0, 0, half), own - half)


def sketch_rows(start, count, fields_ref, edge_ref, mix_ref, store):
    tile, _, width = fields_ref.shape
    columns = width // 3
    for r in range(count):
        layer = fields_ref[start + r]
        if edge_ref is not None and r == 0:
            layer = jnp.where(start == 0, edge_ref[0], layer)
        if edge_ref is not None and r == count - 1:
            layer = jnp.where(start + count == tile, edge_ref[1], layer)
        sketch = jnp.dot(mix_ref[...], layer, preferred_element_type=F32)
        for i in range(3):
            store(r, i, sketch[:, i * columns : (i + 1) * columns])


def send_rows(win, which, fields_ref, edge_ref, mix_ref, send_ref):
    own = fields_ref.shape[0] // win
    for d in range(1, win):
        window = lax.rem(lax.axis_index("win") + d, win)
        offset, count = chunks(window, own)[which]

        def store(r, i, value, d=d):
            send_ref[d - 1, r, i] = value.astype(BF16)

        sketch_rows(window * own + offset, count, fields_ref, edge_ref, mix_ref, store)


def early_kernel(win, fields_ref, mix_ref, send_ref):
    send_rows(win, 0, fields_ref, None, mix_ref, send_ref)


def early_sketch(fields, mix, win):
    tile, _, width = fields.shape
    comps, rank = 3, mix.shape[0]
    return pl.pallas_call(
        lambda *refs: early_kernel(win, *refs),
        out_shape=jax.ShapeDtypeStruct((win - 1, tile // win // 2, comps, rank, width // comps), BF16),
        in_specs=vmem(2),
        out_specs=vmem(1)[0],
        compiler_params=small(14),
        name="early",
    )(fields, mix)


def sketch_kernel(win, turned_ref, fields_ref, far_ref, near_ref, metrics_ref, mix_ref, send_ref, edge_ref):
    comps, tile, snaps, columns = turned_ref.shape
    odd = lax.rem(lax.axis_index("space"), 2) == 1
    one = eta_matrix(columns)
    for side, x in ((0, 0), (1, tile - 1)):
        xi, eta = [], []
        for c in range(comps):
            far, near = far_ref[c].astype(F32), near_ref[c].astype(F32)
            if side:
                upper, lower = jnp.where(odd, far, near), turned_ref[c, x - 1].astype(F32)
            else:
                upper, lower = turned_ref[c, x + 1].astype(F32), jnp.where(odd, near, far)
            xi.append(upper - lower)
            eta.append(jnp.dot(turned_ref[c, x], one, preferred_element_type=F32))
        for i, row in enumerate(field_rows(metrics_ref, x, xi, eta)):
            edge_ref[side, :, i * columns : (i + 1) * columns] = row
    send_rows(win, 1, fields_ref, edge_ref, mix_ref, send_ref)


def sketch_of(turned, fields, far, near, metrics, mix, win):
    comps, tile, snaps, columns = turned.shape
    rank = mix.shape[0]
    own = tile // win - tile // win // 2
    return pl.pallas_call(
        lambda *refs: sketch_kernel(win, *refs),
        out_shape=[
            jax.ShapeDtypeStruct((win - 1, own, comps, rank, columns), BF16),
            jax.ShapeDtypeStruct((2, snaps, comps * columns), BF16),
        ],
        in_specs=vmem(6),
        out_specs=vmem(2),
        compiler_params=small(14),
        name="sketch",
    )(turned, fields, far, near, metrics, mix)


def project_kernel(win, fields_ref, edge_ref, tests_ref, mix_ref, proj_ref, own_ref):
    comps, tile, _, _ = tests_ref.shape
    snaps = fields_ref.shape[1]
    inner = [fields_ref[x] for x in range(1, tile - 1)]
    fields = jnp.concatenate([edge_ref[0], *inner, edge_ref[1]], axis=1)
    tests = jnp.concatenate([tests_ref[c, x] for x in range(tile) for c in range(comps)], axis=1)
    total = lax.dot_general(fields, tests, NT, preferred_element_type=F32)
    half = snaps // 2
    proj_ref[...] = jnp.concatenate([total[:half, :], total[half:, :]], axis=1)
    own = tile // win

    def store(r, i, value):
        own_ref[r, i] = value

    sketch_rows(lax.axis_index("win") * own, own, fields_ref, edge_ref, mix_ref, store)


def project(fields, edges, tests, mix, win):
    tile, snaps, width = fields.shape
    comps, _, rank, columns = tests.shape
    return pl.pallas_call(
        lambda *refs: project_kernel(win, *refs),
        out_shape=[
            jax.ShapeDtypeStruct((snaps // 2, 2 * rank), F32),
            jax.ShapeDtypeStruct((tile // win, comps, rank, columns), F32),
        ],
        in_specs=vmem(4),
        out_specs=vmem(2),
        compiler_params=small(14),
        name="project",
    )(fields, edges, tests, mix)


def gram_part(which, own_ref, got_ref, stack_ref):
    own, comps, rank, columns = own_ref.shape
    offset, count = chunks(lax.axis_index("win"), own)[which]
    for x in range(count):
        for c in range(comps):
            total = own_ref[offset + x, c]
            for d in range(got_ref.shape[0]):
                total = total + got_ref[d, x, c].astype(F32)
            high, low = split(total)
            at = (x * comps + c) * columns
            stack_ref[:rank, at : at + columns] = high
            stack_ref[rank : 2 * rank, at : at + columns] = low
            stack_ref[2 * rank :, at : at + columns] = high
    stack = stack_ref[: 2 * rank, :]
    pair = lax.dot_general(stack, stack, NT, preferred_element_type=F32)
    return pair[:rank, :rank] + pair[:rank, rank:] + pair[rank:, :rank] + pair[rank:, rank:]


def packed(gram, other):
    rank = gram.shape[0]
    row = lax.broadcasted_iota(jnp.int32, (rank, rank), 0)
    col = lax.broadcasted_iota(jnp.int32, (rank, rank), 1)
    both = jnp.where(col >= row, gram, other)
    half = rank // 2
    return jnp.concatenate([both[:half], both[half:]], axis=1)


def first_kernel(own_ref, got_ref, shares_ref, stack_ref, gram_ref):
    rank = own_ref.shape[2]
    gram = gram_part(0, own_ref, got_ref, stack_ref)
    share = shares_ref[0]
    for i in range(1, shares_ref.shape[0]):
        share = share + shares_ref[i]
    pair = lax.dot_general(share, share, TN, precision=EXACT, preferred_element_type=F32)
    other = pair[:rank, :rank] + pair[rank:, rank:]
    row = lax.broadcasted_iota(jnp.int32, (rank, rank), 0)
    col = lax.broadcasted_iota(jnp.int32, (rank, rank), 1)
    half = rank // 2
    gram_ref[:half, :] = packed(gram, other)
    gram_ref[half:, :] = jnp.zeros_like(gram_ref[half:, :])
    gram_ref[half : half + 1, :rank] = jnp.sum(jnp.where(col == row, other, 0.0), axis=0, keepdims=True)


def second_kernel(own_ref, got_ref, part_ref, stack_ref, gram_ref):
    rank = own_ref.shape[2]
    half = rank // 2
    gram = gram_part(1, own_ref, got_ref, stack_ref)
    gram_ref[:half, :] = part_ref[:half, :] + packed(gram, jnp.zeros_like(gram))
    gram_ref[half:, :] = part_ref[half:, :]


def grams_of(kernel, own, got, other, name):
    rows, comps, rank, columns = got.shape[1:]
    return pl.pallas_call(
        kernel,
        out_shape=[
            jax.ShapeDtypeStruct((3 * rank, rows * comps * columns), BF16),
            jax.ShapeDtypeStruct((rank // 2 + 8, 2 * rank), F32),
        ],
        in_specs=vmem(3),
        out_specs=vmem(2),
        compiler_params=small(16),
        name=name,
    )(own, got, other)


def finish_kernel(cells, snaps, gram_ref, first_ref, second_ref, q_ref, r_range_ref, r_corange_ref, wide_r, wide_c, factors_ref, out_ref, sems):
    rank = wide_r.shape[0]
    row = lax.broadcasted_iota(jnp.int32, (rank, rank), 0)
    col = lax.broadcasted_iota(jnp.int32, (rank, rank), 1)
    eye = (row == col).astype(F32)
    held = (wide_r, wide_c)

    def save(m, r, value):
        held[m][r : r + 1, :] = value

    half = rank // 2
    both = jnp.concatenate([gram_ref[:half, :rank], gram_ref[:half, rank:]], axis=0)
    turned = both.T
    diagonal = gram_ref[half : half + 1, :rank]
    gram = jnp.where(col >= row, both, turned)
    other = jnp.where(col == row, diagonal, jnp.where(col > row, turned, both))
    pair = (gram / cells, other / snaps)
    chains = [jnp.concatenate([g, eye], axis=1) for g in pair]
    eliminate(chains, 8 if rank % 8 == 0 else 1, save)
    factors_ref[0] = jnp.where(col >= row, wide_r[:, :rank], 0.0)
    factors_ref[1] = jnp.where(col >= row, wide_c[:, :rank], 0.0)
    leaving = [
        pltpu.make_async_copy(factors_ref.at[i], ref, sems.at[out_ref.shape[0] + i])
        for i, ref in enumerate((r_range_ref, r_corange_ref))
    ]
    for copy in leaving:
        copy.start()
    high, low = split(jnp.where(col <= row, wide_r[:, rank:], 0.0))
    left = jnp.concatenate([high, high, low], axis=1)
    own, comps, _, columns = out_ref.shape
    width = comps * columns
    copies = []
    runs = chunks(lax.axis_index("win"), own)
    for stack_ref, (offset, count) in zip((first_ref, second_ref), runs):
        for r in range(count):
            at = len(copies)
            right = stack_ref[:, r * width : (r + 1) * width]
            value = jnp.dot(left, right, preferred_element_type=F32)
            for c in range(comps):
                out_ref[at, c] = value[:, c * columns : (c + 1) * columns]
            copies.append(pltpu.make_async_copy(out_ref.at[at], q_ref.at[offset + r], sems.at[at]))
            copies[-1].start()
    for copy in copies:
        copy.wait()
    for copy in leaving:
        copy.wait()


def finish(gram, first, second, shape, cells, snaps):
    rank = shape[2]
    square = jax.ShapeDtypeStruct((rank, rank), F32)
    return pl.pallas_call(
        lambda *refs: finish_kernel(cells, snaps, *refs),
        out_shape=[jax.ShapeDtypeStruct(shape, F32), square, square],
        in_specs=vmem(3),
        out_specs=[pl.BlockSpec(memory_space=pl.ANY)] * 3,
        scratch_shapes=[
            *[pltpu.VMEM((rank, 2 * rank), F32)] * 2,
            pltpu.VMEM((2, rank, rank), F32),
            pltpu.VMEM(shape, F32),
            pltpu.SemaphoreType.DMA((shape[0] + 2,)),
        ],
        compiler_params=small(16),
        name="finish",
    )(gram, first, second)


def swapped(edges):
    count = lax.axis_size("space")
    across = [(i, i + 1) for i in range(1, count - 1, 2)]
    within = [(i, i + 1) for i in range(0, count - 1, 2)]
    far = lax.ppermute(edges[0], "space", across + [(j, i) for i, j in across])
    near = lax.ppermute(edges[1], "space", within + [(j, i) for i, j in within])
    return far, near


def body(snapshots, metrics, range_test, corange_test):
    space, win = lax.axis_size("space"), lax.axis_size("win")
    snaps, comps, tile, columns = snapshots.shape
    rank = range_test.shape[1]
    turned = jnp.transpose(snapshots, (1, 2, 0, 3))
    far, near = swapped(edges_of(turned))
    fields = inner_fields(turned, metrics)
    early = early_sketch(fields, range_test.T, win)
    send, edges = sketch_of(turned, fields, far, near, metrics, range_test.T, win)
    got = [[], []]
    for which, rows in enumerate((early, send)):
        for d in range(1, win):
            ring = [(i, (i + d) % win) for i in range(win)]
            got[which].append(lax.ppermute(rows[d - 1], "win", ring))
    projection, own = project(fields, edges, jnp.transpose(corange_test, (1, 2, 0, 3)), range_test.T, win)
    shares = projection.reshape(space, snaps // 2 // space, 2 * rank)
    shares = lax.all_to_all(shares, "space", 0, 0, tiled=True)
    first, gram = grams_of(first_kernel, own, jnp.stack(got[0]), shares, "first")
    second, gram = grams_of(second_kernel, own, jnp.stack(got[1]), gram, "second")
    gram = total_over_all(gram)
    q_turned, r_range, r_corange = finish(
        gram, first, second, own.shape, comps * tile * space * columns, snaps * win
    )
    return (jnp.transpose(q_turned, (0, 2, 1, 3)), r_range, r_corange)


def solution(mesh):
    placed = (
        P("win", None, "space", None),
        P(None, "space", None),
        P("win", None),
        P(None, None, "space", None),
    )
    return jax.shard_map(
        body,
        mesh=mesh,
        in_specs=placed,
        out_specs=(P(("space", "win"), None, None, None), P(), P()),
        check_vma=False,
    )
```

```python
import jax
import jax.numpy as jnp
from jax import lax
from jax.experimental import pallas as pl
from jax.experimental.pallas import tpu as pltpu
from jax.sharding import PartitionSpec as P

BOTH = ("space", "win")
EXACT = lax.Precision.HIGHEST


def hops(space, win):
    space_bits = [win << b for b in range(space.bit_length() - 1)]
    win_bits = [1 << b for b in range(win.bit_length() - 1)]
    stages = [space_bits[:1], win_bits[:1] + space_bits[1:2]]
    rest = win_bits[1:] + space_bits[2:]
    stages += [rest[i : i + 2] for i in range(0, len(rest), 2)]
    return [s for s in stages if s]


def total_over_all(value):
    space, win = lax.axis_size("space"), lax.axis_size("win")
    count = space * win
    if count & (count - 1) or win & (win - 1):
        return lax.psum(value, BOTH)
    for bits in hops(space, win):
        parts = {0: value}
        for b in bits:
            for mask in list(parts):
                pairs = [(i, i ^ mask ^ b) for i in range(count)]
                parts[mask ^ b] = lax.ppermute(value, BOTH, pairs)
        for b in bits:
            parts = {m: parts[m] + parts[m ^ b] for m in parts if not m & b}
        value = parts[0]
    return value


def eliminate(chains, step, save):
    order = chains[0].shape[0]
    for j in range(0, order, step):
        for m, rest in enumerate(chains):
            cols = [jnp.broadcast_to(rest[:, j + a : j + a + 1], rest.shape) for a in range(step)]
            rows = [rest[a : a + 1, :] for a in range(step)]
            rest = rest[step:, :]
            for a in range(step):
                pivot = cols[a][a : a + 1, :]
                scaled = rows[a] / pivot
                for c in range(a + 1, step):
                    ratio = cols[c][a : a + 1, :] / pivot
                    down = cols[a][c : c + 1, :]
                    cols[c] = cols[c] - cols[a] * ratio
                    rows[c] = rows[c] - scaled * down
                save(m, j + a, rows[a] * lax.rsqrt(pivot))
                if j + step < order:
                    rest = rest - cols[a][step:, :] * scaled
            chains[m] = rest


NT = (((1,), (1,)), ((), ()))
TN = (((0,), (0,)), ((), ()))
F32, BF16 = jnp.float32, jnp.bfloat16


def vmem(count):
    return [pl.BlockSpec(memory_space=pltpu.VMEM)] * count


def small(limit):
    return pltpu.CompilerParams(vmem_limit_bytes=limit << 20)


def split(value):
    high = value.astype(BF16)
    return high, (value - high.astype(F32)).astype(BF16)


def edge_kernel(turned_ref, edges_ref):
    tile = turned_ref.shape[1]
    odd = lax.rem(lax.axis_index("space"), 2)
    edges_ref[0] = turned_ref[:, odd * (tile - 1)]
    edges_ref[1] = turned_ref[:, (1 - odd) * (tile - 1)]


def edges_of(turned):
    comps, tile, snaps, columns = turned.shape
    return pl.pallas_call(
        edge_kernel,
        out_shape=jax.ShapeDtypeStruct((2, comps, snaps, columns), BF16),
        in_specs=vmem(1),
        out_specs=vmem(1)[0],
        compiler_params=small(8),
        name="edges",
    )(turned)


def eta_matrix(columns):
    before = lax.broadcasted_iota(jnp.int32, (columns, columns), 0)
    after = lax.broadcasted_iota(jnp.int32, (columns, columns), 1)
    return ((before == after + 1).astype(F32) - (before == after - 1).astype(F32)).astype(BF16)


def field_rows(metrics_ref, x, xi, eta):
    a, b, c, e = [metrics_ref[i, x : x + 1, :] * 0.5 for i in range(4)]
    vortex = a * xi[1] + b * eta[1] - c * xi[0] - e * eta[0]
    rows = [vortex, a * xi[2] + b * eta[2], c * xi[2] + e * eta[2]]
    return [row.astype(BF16) for row in rows]


def inner_kernel(turned_ref, metrics_ref, fields_ref, eta_ref):
    comps, tile, snaps, columns = turned_ref.shape
    half = snaps // 2
    one = eta_matrix(columns)
    none = jnp.zeros_like(one)
    pair = jnp.concatenate(
        [jnp.concatenate([one, none], axis=1), jnp.concatenate([none, one], axis=1)], axis=0
    )
    here = jnp.concatenate([turned_ref[:, :, :half, :], turned_ref[:, :, half:, :]], axis=3)
    here = here.reshape(comps * tile * half, 2 * columns)
    eta_ref[...] = jnp.dot(here, pair, preferred_element_type=F32)
    part = min(half, 32)
    for s in range(0, snaps, part):
        lane = s // half * columns

        def layer(x):
            return [turned_ref[c, x, s : s + part, :].astype(F32) for c in range(comps)]

        below, level = layer(0), layer(1)
        for x in range(1, tile - 1):
            above = layer(x + 1)
            xi = [up - down for up, down in zip(above, below)]
            at = [(c * tile + x) * half + s % half for c in range(comps)]
            eta = [eta_ref[i : i + part, lane : lane + columns] for i in at]
            for i, row in enumerate(field_rows(metrics_ref, x, xi, eta)):
                fields_ref[x, s : s + part, i * columns : (i + 1) * columns] = row
            below, level = level, above


def inner_fields(turned, metrics):
    comps, tile, snaps, columns = turned.shape
    return pl.pallas_call(
        inner_kernel,
        out_shape=jax.ShapeDtypeStruct((tile, snaps, comps * columns), BF16),
        in_specs=vmem(2),
        out_specs=vmem(1)[0],
        scratch_shapes=[pltpu.VMEM((comps * tile * snaps // 2, 2 * columns), F32)],
        compiler_params=small(14),
        cost_estimate=pl.CostEstimate(flops=10**9, bytes_accessed=4 * 10**6, transcendentals=0),
        name="inner",
    )(turned, metrics)


def chunks(window, own):
    half = own // 2
    return (jnp.where(window == 0, own - half, 0), half), (jnp.where(window == 0, 0, half), own - half)


def sketch_rows(start, count, fields_ref, edge_ref, mix_ref, store):
    tile, _, width = fields_ref.shape
    columns = width // 3
    for r in range(count):
        layer = fields_ref[start + r]
        if edge_ref is not None and r == 0:
            layer = jnp.where(start == 0, edge_ref[0], layer)
        if edge_ref is not None and r == count - 1:
            layer = jnp.where(start + count == tile, edge_ref[1], layer)
        sketch = jnp.dot(mix_ref[...], layer, preferred_element_type=F32)
        for i in range(3):
            store(r, i, sketch[:, i * columns : (i + 1) * columns])


def send_rows(win, which, fields_ref, edge_ref, mix_ref, send_ref):
    own = fields_ref.shape[0] // win
    for d in range(1, win):
        window = lax.rem(lax.axis_index("win") + d, win)
        offset, count = chunks(window, own)[which]

        def store(r, i, value, d=d):
            send_ref[d - 1, r, i] = value.astype(BF16)

        sketch_rows(window * own + offset, count, fields_ref, edge_ref, mix_ref, store)


def early_kernel(win, fields_ref, mix_ref, send_ref):
    send_rows(win, 0, fields_ref, None, mix_ref, send_ref)


def early_sketch(fields, mix, win):
    tile, _, width = fields.shape
    comps, rank = 3, mix.shape[0]
    return pl.pallas_call(
        lambda *refs: early_kernel(win, *refs),
        out_shape=jax.ShapeDtypeStruct((win - 1, tile // win // 2, comps, rank, width // comps), BF16),
        in_specs=vmem(2),
        out_specs=vmem(1)[0],
        compiler_params=small(14),
        name="early",
    )(fields, mix)


def sketch_kernel(win, turned_ref, fields_ref, far_ref, near_ref, metrics_ref, mix_ref, send_ref, edge_ref):
    comps, tile, snaps, columns = turned_ref.shape
    odd = lax.rem(lax.axis_index("space"), 2) == 1
    one = eta_matrix(columns)
    for side, x in ((0, 0), (1, tile - 1)):
        xi, eta = [], []
        for c in range(comps):
            far, near = far_ref[c].astype(F32), near_ref[c].astype(F32)
            if side:
                upper, lower = jnp.where(odd, far, near), turned_ref[c, x - 1].astype(F32)
            else:
                upper, lower = turned_ref[c, x + 1].astype(F32), jnp.where(odd, near, far)
            xi.append(upper - lower)
            eta.append(jnp.dot(turned_ref[c, x], one, preferred_element_type=F32))
        for i, row in enumerate(field_rows(metrics_ref, x, xi, eta)):
            edge_ref[side, :, i * columns : (i + 1) * columns] = row
    send_rows(win, 1, fields_ref, edge_ref, mix_ref, send_ref)


def sketch_of(turned, fields, far, near, metrics, mix, win):
    comps, tile, snaps, columns = turned.shape
    rank = mix.shape[0]
    own = tile // win - tile // win // 2
    return pl.pallas_call(
        lambda *refs: sketch_kernel(win, *refs),
        out_shape=[
            jax.ShapeDtypeStruct((win - 1, own, comps, rank, columns), BF16),
            jax.ShapeDtypeStruct((2, snaps, comps * columns), BF16),
        ],
        in_specs=vmem(6),
        out_specs=vmem(2),
        compiler_params=small(14),
        name="sketch",
    )(turned, fields, far, near, metrics, mix)


def project_kernel(win, fields_ref, edge_ref, tests_ref, mix_ref, proj_ref, own_ref):
    comps, tile, _, _ = tests_ref.shape
    snaps = fields_ref.shape[1]
    inner = [fields_ref[x] for x in range(1, tile - 1)]
    fields = jnp.concatenate([edge_ref[0], *inner, edge_ref[1]], axis=1)
    tests = jnp.concatenate([tests_ref[c, x] for x in range(tile) for c in range(comps)], axis=1)
    total = lax.dot_general(fields, tests, NT, preferred_element_type=F32)
    half = snaps // 2
    proj_ref[...] = jnp.concatenate([total[:half, :], total[half:, :]], axis=1)
    own = tile // win

    def store(r, i, value):
        own_ref[r, i] = value

    sketch_rows(lax.axis_index("win") * own, own, fields_ref, edge_ref, mix_ref, store)


def project(fields, edges, tests, mix, win):
    tile, snaps, width = fields.shape
    comps, _, rank, columns = tests.shape
    return pl.pallas_call(
        lambda *refs: project_kernel(win, *refs),
        out_shape=[
            jax.ShapeDtypeStruct((snaps // 2, 2 * rank), F32),
            jax.ShapeDtypeStruct((tile // win, comps, rank, columns), F32),
        ],
        in_specs=vmem(4),
        out_specs=vmem(2),
        compiler_params=small(14),
        name="project",
    )(fields, edges, tests, mix)


def gram_kernel(own_ref, early_ref, late_ref, shares_ref, stack_ref, gram_ref):
    own, comps, rank, columns = own_ref.shape
    at = 0
    for got_ref, (offset, count) in zip((early_ref, late_ref), chunks(lax.axis_index("win"), own)):
        for x in range(count):
            for c in range(comps):
                total = own_ref[offset + x, c]
                for d in range(got_ref.shape[0]):
                    total = total + got_ref[d, x, c].astype(F32)
                high, low = split(total)
                stack_ref[:rank, at : at + columns] = high
                stack_ref[rank : 2 * rank, at : at + columns] = low
                stack_ref[2 * rank :, at : at + columns] = high
                at += columns
    stack = stack_ref[: 2 * rank, :]
    pair = lax.dot_general(stack, stack, NT, preferred_element_type=F32)
    gram = pair[:rank, :rank] + pair[:rank, rank:] + pair[rank:, :rank] + pair[rank:, rank:]
    share = shares_ref[0]
    for i in range(1, shares_ref.shape[0]):
        share = share + shares_ref[i]
    pair = lax.dot_general(share, share, TN, precision=EXACT, preferred_element_type=F32)
    other = pair[:rank, :rank] + pair[rank:, rank:]
    row = lax.broadcasted_iota(jnp.int32, (rank, rank), 0)
    col = lax.broadcasted_iota(jnp.int32, (rank, rank), 1)
    half = rank // 2
    gram_ref[:half, :] = packed(gram, other)
    gram_ref[half:, :] = jnp.zeros_like(gram_ref[half:, :])
    gram_ref[half : half + 1, :rank] = jnp.sum(jnp.where(col == row, other, 0.0), axis=0, keepdims=True)


def packed(gram, other):
    rank = gram.shape[0]
    row = lax.broadcasted_iota(jnp.int32, (rank, rank), 0)
    col = lax.broadcasted_iota(jnp.int32, (rank, rank), 1)
    both = jnp.where(col >= row, gram, other)
    half = rank // 2
    return jnp.concatenate([both[:half], both[half:]], axis=1)


def grams_of(own, early, late, shares):
    rows, comps, rank, columns = own.shape
    return pl.pallas_call(
        gram_kernel,
        out_shape=[
            jax.ShapeDtypeStruct((3 * rank, rows * comps * columns), BF16),
            jax.ShapeDtypeStruct((rank // 2 + 8, 2 * rank), F32),
        ],
        in_specs=vmem(4),
        out_specs=vmem(2),
        compiler_params=small(16),
        name="grams",
    )(own, early, late, shares)


def finish_kernel(cells, snaps, gram_ref, stack_ref, q_ref, r_range_ref, r_corange_ref, wide_r, wide_c, factors_ref, out_ref, sems):
    rank = wide_r.shape[0]
    row = lax.broadcasted_iota(jnp.int32, (rank, rank), 0)
    col = lax.broadcasted_iota(jnp.int32, (rank, rank), 1)
    eye = (row == col).astype(F32)
    held = (wide_r, wide_c)

    def save(m, r, value):
        held[m][r : r + 1, :] = value

    half = rank // 2
    both = jnp.concatenate([gram_ref[:half, :rank], gram_ref[:half, rank:]], axis=0)
    turned = both.T
    diagonal = gram_ref[half : half + 1, :rank]
    gram = jnp.where(col >= row, both, turned)
    other = jnp.where(col == row, diagonal, jnp.where(col > row, turned, both))
    pair = (gram / cells, other / snaps)
    chains = [jnp.concatenate([g, eye], axis=1) for g in pair]
    eliminate(chains, 8 if rank % 8 == 0 else 1, save)
    factors_ref[0] = jnp.where(col >= row, wide_r[:, :rank], 0.0)
    factors_ref[1] = jnp.where(col >= row, wide_c[:, :rank], 0.0)
    leaving = [
        pltpu.make_async_copy(factors_ref.at[i], ref, sems.at[out_ref.shape[0] + i])
        for i, ref in enumerate((r_range_ref, r_corange_ref))
    ]
    for copy in leaving:
        copy.start()
    high, low = split(jnp.where(col <= row, wide_r[:, rank:], 0.0))
    left = jnp.concatenate([high, high, low], axis=1)
    own, comps, _, columns = out_ref.shape
    width = comps * columns
    copies = []
    runs = chunks(lax.axis_index("win"), own)
    for offset, count in runs:
        for r in range(count):
            at = len(copies)
            right = stack_ref[:, at * width : (at + 1) * width]
            value = jnp.dot(left, right, preferred_element_type=F32)
            for c in range(comps):
                out_ref[at, c] = value[:, c * columns : (c + 1) * columns]
            copies.append(pltpu.make_async_copy(out_ref.at[at], q_ref.at[offset + r], sems.at[at]))
            copies[-1].start()
    for copy in copies:
        copy.wait()
    for copy in leaving:
        copy.wait()


def finish(gram, stack, shape, cells, snaps):
    rank = shape[2]
    square = jax.ShapeDtypeStruct((rank, rank), F32)
    return pl.pallas_call(
        lambda *refs: finish_kernel(cells, snaps, *refs),
        out_shape=[jax.ShapeDtypeStruct(shape, F32), square, square],
        in_specs=vmem(2),
        out_specs=[pl.BlockSpec(memory_space=pl.ANY)] * 3,
        scratch_shapes=[
            *[pltpu.VMEM((rank, 2 * rank), F32)] * 2,
            pltpu.VMEM((2, rank, rank), F32),
            pltpu.VMEM(shape, F32),
            pltpu.SemaphoreType.DMA((shape[0] + 2,)),
        ],
        compiler_params=small(16),
        name="finish",
    )(gram, stack)


def swapped(edges):
    count = lax.axis_size("space")
    across = [(i, i + 1) for i in range(1, count - 1, 2)]
    within = [(i, i + 1) for i in range(0, count - 1, 2)]
    far = lax.ppermute(edges[0], "space", across + [(j, i) for i, j in across])
    near = lax.ppermute(edges[1], "space", within + [(j, i) for i, j in within])
    return far, near


def body(snapshots, metrics, range_test, corange_test):
    space, win = lax.axis_size("space"), lax.axis_size("win")
    snaps, comps, tile, columns = snapshots.shape
    rank = range_test.shape[1]
    turned = jnp.transpose(snapshots, (1, 2, 0, 3))
    far, near = swapped(edges_of(turned))
    fields = inner_fields(turned, metrics)
    early = early_sketch(fields, range_test.T, win)
    send, edges = sketch_of(turned, fields, far, near, metrics, range_test.T, win)
    got = [[], []]
    for which, rows in enumerate((early, send)):
        for d in range(1, win):
            ring = [(i, (i + d) % win) for i in range(win)]
            got[which].append(lax.ppermute(rows[d - 1], "win", ring))
    projection, own = project(fields, edges, jnp.transpose(corange_test, (1, 2, 0, 3)), range_test.T, win)
    shares = projection.reshape(space, snaps // 2 // space, 2 * rank)
    shares = lax.all_to_all(shares, "space", 0, 0, tiled=True)
    stack, gram = grams_of(own, jnp.stack(got[0]), jnp.stack(got[1]), shares)
    gram = total_over_all(gram)
    q_turned, r_range, r_corange = finish(
        gram, stack, own.shape, comps * tile * space * columns, snaps * win
    )
    return (jnp.transpose(q_turned, (0, 2, 1, 3)), r_range, r_corange)


def solution(mesh):
    placed = (
        P("win", None, "space", None),
        P(None, "space", None),
        P("win", None),
        P(None, None, "space", None),
    )
    return jax.shard_map(
        body,
        mesh=mesh,
        in_specs=placed,
        out_specs=(P(("space", "win"), None, None, None), P(), P()),
        check_vma=False,
    )
```

```python
import jax
import jax.numpy as jnp
from jax import lax
from jax.experimental import pallas as pl
from jax.experimental.pallas import tpu as pltpu
from jax.sharding import PartitionSpec as P

BOTH = ("space", "win")
EXACT = lax.Precision.HIGHEST


def hops(space, win):
    space_bits = [win << b for b in range(space.bit_length() - 1)]
    win_bits = [1 << b for b in range(win.bit_length() - 1)]
    stages = [space_bits[:1], win_bits[:1] + space_bits[1:2]]
    rest = win_bits[1:] + space_bits[2:]
    stages += [rest[i : i + 2] for i in range(0, len(rest), 2)]
    return [s for s in stages if s]


def total_over_all(value):
    space, win = lax.axis_size("space"), lax.axis_size("win")
    count = space * win
    if count & (count - 1) or win & (win - 1):
        return lax.psum(value, BOTH)
    for bits in hops(space, win):
        parts = {0: value}
        for b in bits:
            for mask in list(parts):
                pairs = [(i, i ^ mask ^ b) for i in range(count)]
                parts[mask ^ b] = lax.ppermute(value, BOTH, pairs)
        for b in bits:
            parts = {m: parts[m] + parts[m ^ b] for m in parts if not m & b}
        value = parts[0]
    return value


def eliminate(pair, step, save):
    order, width = pair.shape
    rest = pair
    for j in range(0, order, step):
        count = rest.shape[0]
        lane = lax.broadcasted_iota(jnp.int32, (count, width), 1)
        side = jnp.where(lane < order, 0, order)
        here = lane - side
        cols = [jnp.take_along_axis(rest, side + (j + a), axis=1) for a in range(step)]
        spot = here[:1]
        inside = (spot >= j) & (spot < j + step)
        rows = [
            jnp.where(inside, jnp.where(spot == j + a, 1.0, 0.0), rest[a : a + 1, :]) for a in range(step)
        ]
        rest = jnp.where((here >= j) & (here < j + step), 0.0, rest)[step:, :]
        for a in range(step):
            pivot = cols[a][a : a + 1, :]
            root = lax.rsqrt(pivot)
            upper = jnp.where(spot == j + a, pivot, rows[a])
            for c in range(a + 1, step):
                upper = jnp.where(spot == j + c, cols[c][a : a + 1, :], upper)
            save(j + a, upper * root, rows[a] * root)
            scaled = rows[a] / pivot
            for c in range(a + 1, step):
                ratio = cols[c][a : a + 1, :] / pivot
                down = cols[a][c : c + 1, :]
                cols[c] = cols[c] - cols[a] * ratio
                rows[c] = rows[c] - scaled * down
            if j + step < order:
                rest = rest - cols[a][step:, :] * scaled


NT = (((1,), (1,)), ((), ()))
TN = (((0,), (0,)), ((), ()))
F32, BF16 = jnp.float32, jnp.bfloat16


def vmem(count):
    return [pl.BlockSpec(memory_space=pltpu.VMEM)] * count


def small(limit):
    return pltpu.CompilerParams(vmem_limit_bytes=limit << 20)


def split(value):
    high = value.astype(BF16)
    return high, (value - high.astype(F32)).astype(BF16)


def edge_kernel(turned_ref, edges_ref):
    tile = turned_ref.shape[1]
    odd = lax.rem(lax.axis_index("space"), 2)
    edges_ref[0] = turned_ref[:, odd * (tile - 1)]
    edges_ref[1] = turned_ref[:, (1 - odd) * (tile - 1)]


def edges_of(turned):
    comps, tile, snaps, columns = turned.shape
    return pl.pallas_call(
        edge_kernel,
        out_shape=jax.ShapeDtypeStruct((2, comps, snaps, columns), BF16),
        in_specs=vmem(1),
        out_specs=vmem(1)[0],
        compiler_params=small(8),
        name="edges",
    )(turned)


def eta_matrix(columns):
    before = lax.broadcasted_iota(jnp.int32, (columns, columns), 0)
    after = lax.broadcasted_iota(jnp.int32, (columns, columns), 1)
    return ((before == after + 1).astype(F32) - (before == after - 1).astype(F32)).astype(BF16)


def field_rows(metrics_ref, x, xi, eta):
    a, b, c, e = [metrics_ref[i, x : x + 1, :] * 0.5 for i in range(4)]
    vortex = a * xi[1] + b * eta[1] - c * xi[0] - e * eta[0]
    rows = [vortex, a * xi[2] + b * eta[2], c * xi[2] + e * eta[2]]
    return [row.astype(BF16) for row in rows]


def inner_kernel(turned_ref, metrics_ref, fields_ref, eta_ref):
    comps, tile, snaps, columns = turned_ref.shape
    half = snaps // 2
    one = eta_matrix(columns)
    none = jnp.zeros_like(one)
    pair = jnp.concatenate(
        [jnp.concatenate([one, none], axis=1), jnp.concatenate([none, one], axis=1)], axis=0
    )
    here = jnp.concatenate([turned_ref[:, :, :half, :], turned_ref[:, :, half:, :]], axis=3)
    here = here.reshape(comps * tile * half, 2 * columns)
    eta_ref[...] = jnp.dot(here, pair, preferred_element_type=F32)
    part = min(half, 32)
    for s in range(0, snaps, part):
        lane = s // half * columns

        def layer(x):
            return [turned_ref[c, x, s : s + part, :].astype(F32) for c in range(comps)]

        below, level = layer(0), layer(1)
        for x in range(1, tile - 1):
            above = layer(x + 1)
            xi = [up - down for up, down in zip(above, below)]
            at = [(c * tile + x) * half + s % half for c in range(comps)]
            eta = [eta_ref[i : i + part, lane : lane + columns] for i in at]
            for i, row in enumerate(field_rows(metrics_ref, x, xi, eta)):
                fields_ref[x, s : s + part, i * columns : (i + 1) * columns] = row
            below, level = level, above


def inner_fields(turned, metrics):
    comps, tile, snaps, columns = turned.shape
    return pl.pallas_call(
        inner_kernel,
        out_shape=jax.ShapeDtypeStruct((tile, snaps, comps * columns), BF16),
        in_specs=vmem(2),
        out_specs=vmem(1)[0],
        scratch_shapes=[pltpu.VMEM((comps * tile * snaps // 2, 2 * columns), F32)],
        compiler_params=small(14),
        cost_estimate=pl.CostEstimate(flops=10**9, bytes_accessed=4 * 10**6, transcendentals=0),
        name="inner",
    )(turned, metrics)


def chunks(window, own):
    half = own // 2
    return (jnp.where(window == 0, own - half, 0), half), (jnp.where(window == 0, 0, half), own - half)


def sketch_rows(start, count, fields_ref, edge_ref, mix_ref, store):
    tile, _, width = fields_ref.shape
    columns = width // 3
    for r in range(count):
        layer = fields_ref[start + r]
        if edge_ref is not None and r == 0:
            layer = jnp.where(start == 0, edge_ref[0], layer)
        if edge_ref is not None and r == count - 1:
            layer = jnp.where(start + count == tile, edge_ref[1], layer)
        sketch = jnp.dot(mix_ref[...], layer, preferred_element_type=F32)
        for i in range(3):
            store(r, i, sketch[:, i * columns : (i + 1) * columns])


def send_rows(win, which, fields_ref, edge_ref, mix_ref, send_ref):
    own = fields_ref.shape[0] // win
    for d in range(1, win):
        window = lax.rem(lax.axis_index("win") + d, win)
        offset, count = chunks(window, own)[which]

        def store(r, i, value, d=d):
            send_ref[d - 1, r, i] = value.astype(BF16)

        sketch_rows(window * own + offset, count, fields_ref, edge_ref, mix_ref, store)


def early_kernel(win, fields_ref, mix_ref, send_ref):
    send_rows(win, 0, fields_ref, None, mix_ref, send_ref)


def early_sketch(fields, mix, win):
    tile, _, width = fields.shape
    comps, rank = 3, mix.shape[0]
    return pl.pallas_call(
        lambda *refs: early_kernel(win, *refs),
        out_shape=jax.ShapeDtypeStruct((win - 1, tile // win // 2, comps, rank, width // comps), BF16),
        in_specs=vmem(2),
        out_specs=vmem(1)[0],
        compiler_params=small(14),
        name="early",
    )(fields, mix)


def sketch_kernel(win, turned_ref, fields_ref, far_ref, near_ref, metrics_ref, mix_ref, send_ref, edge_ref):
    comps, tile, snaps, columns = turned_ref.shape
    odd = lax.rem(lax.axis_index("space"), 2) == 1
    one = eta_matrix(columns)
    for side, x in ((0, 0), (1, tile - 1)):
        xi, eta = [], []
        for c in range(comps):
            far, near = far_ref[c].astype(F32), near_ref[c].astype(F32)
            if side:
                upper, lower = jnp.where(odd, far, near), turned_ref[c, x - 1].astype(F32)
            else:
                upper, lower = turned_ref[c, x + 1].astype(F32), jnp.where(odd, near, far)
            xi.append(upper - lower)
            eta.append(jnp.dot(turned_ref[c, x], one, preferred_element_type=F32))
        for i, row in enumerate(field_rows(metrics_ref, x, xi, eta)):
            edge_ref[side, :, i * columns : (i + 1) * columns] = row
    send_rows(win, 1, fields_ref, edge_ref, mix_ref, send_ref)


def sketch_of(turned, fields, far, near, metrics, mix, win):
    comps, tile, snaps, columns = turned.shape
    rank = mix.shape[0]
    own = tile // win - tile // win // 2
    return pl.pallas_call(
        lambda *refs: sketch_kernel(win, *refs),
        out_shape=[
            jax.ShapeDtypeStruct((win - 1, own, comps, rank, columns), BF16),
            jax.ShapeDtypeStruct((2, snaps, comps * columns), BF16),
        ],
        in_specs=vmem(6),
        out_specs=vmem(2),
        compiler_params=small(14),
        name="sketch",
    )(turned, fields, far, near, metrics, mix)


def project_kernel(win, fields_ref, edge_ref, tests_ref, mix_ref, proj_ref, own_ref):
    comps, tile, _, _ = tests_ref.shape
    snaps = fields_ref.shape[1]
    inner = [fields_ref[x] for x in range(1, tile - 1)]
    fields = jnp.concatenate([edge_ref[0], *inner, edge_ref[1]], axis=1)
    tests = jnp.concatenate([tests_ref[c, x] for x in range(tile) for c in range(comps)], axis=1)
    total = lax.dot_general(fields, tests, NT, preferred_element_type=F32)
    half = snaps // 2
    proj_ref[...] = jnp.concatenate([total[:half, :], total[half:, :]], axis=1)
    own = tile // win

    def store(r, i, value):
        own_ref[r, i] = value

    sketch_rows(lax.axis_index("win") * own, own, fields_ref, edge_ref, mix_ref, store)


def project(fields, edges, tests, mix, win):
    tile, snaps, width = fields.shape
    comps, _, rank, columns = tests.shape
    return pl.pallas_call(
        lambda *refs: project_kernel(win, *refs),
        out_shape=[
            jax.ShapeDtypeStruct((snaps // 2, 2 * rank), F32),
            jax.ShapeDtypeStruct((tile // win, comps, rank, columns), F32),
        ],
        in_specs=vmem(4),
        out_specs=vmem(2),
        compiler_params=small(14),
        name="project",
    )(fields, edges, tests, mix)


def gram_kernel(own_ref, early_ref, late_ref, shares_ref, stack_ref, gram_ref):
    own, comps, rank, columns = own_ref.shape
    at = 0
    for got_ref, (offset, count) in zip((early_ref, late_ref), chunks(lax.axis_index("win"), own)):
        for x in range(count):
            for c in range(comps):
                total = own_ref[offset + x, c]
                for d in range(got_ref.shape[0]):
                    total = total + got_ref[d, x, c].astype(F32)
                high, low = split(total)
                stack_ref[:rank, at : at + columns] = high
                stack_ref[rank : 2 * rank, at : at + columns] = low
                stack_ref[2 * rank :, at : at + columns] = high
                at += columns
    stack = stack_ref[: 2 * rank, :]
    pair = lax.dot_general(stack, stack, NT, preferred_element_type=F32)
    gram = pair[:rank, :rank] + pair[:rank, rank:] + pair[rank:, :rank] + pair[rank:, rank:]
    share = shares_ref[0]
    for i in range(1, shares_ref.shape[0]):
        share = share + shares_ref[i]
    pair = lax.dot_general(share, share, TN, precision=EXACT, preferred_element_type=F32)
    other = pair[:rank, :rank] + pair[rank:, rank:]
    row = lax.broadcasted_iota(jnp.int32, (rank, rank), 0)
    col = lax.broadcasted_iota(jnp.int32, (rank, rank), 1)
    half = rank // 2
    gram_ref[:half, :] = packed(gram, other)
    gram_ref[half:, :] = jnp.zeros_like(gram_ref[half:, :])
    gram_ref[half : half + 1, :rank] = jnp.sum(jnp.where(col == row, other, 0.0), axis=0, keepdims=True)


def packed(gram, other):
    rank = gram.shape[0]
    row = lax.broadcasted_iota(jnp.int32, (rank, rank), 0)
    col = lax.broadcasted_iota(jnp.int32, (rank, rank), 1)
    both = jnp.where(col >= row, gram, other)
    half = rank // 2
    return jnp.concatenate([both[:half], both[half:]], axis=1)


def grams_of(own, early, late, shares):
    rows, comps, rank, columns = own.shape
    return pl.pallas_call(
        gram_kernel,
        out_shape=[
            jax.ShapeDtypeStruct((3 * rank, rows * comps * columns), BF16),
            jax.ShapeDtypeStruct((rank // 2 + 8, 2 * rank), F32),
        ],
        in_specs=vmem(4),
        out_specs=vmem(2),
        compiler_params=small(16),
        name="grams",
    )(own, early, late, shares)


def finish_kernel(cells, snaps, gram_ref, stack_ref, q_ref, r_range_ref, r_corange_ref, upper_ref, lower_ref, factors_ref, out_ref, sems):
    rank = upper_ref.shape[0]
    row = lax.broadcasted_iota(jnp.int32, (rank, rank), 0)
    col = lax.broadcasted_iota(jnp.int32, (rank, rank), 1)

    def save(r, upper, lower):
        upper_ref[r : r + 1, :] = upper
        lower_ref[r : r + 1, :] = lower

    half = rank // 2
    both = jnp.concatenate([gram_ref[:half, :rank], gram_ref[:half, rank:]], axis=0)
    turned = both.T
    diagonal = gram_ref[half : half + 1, :rank]
    gram = jnp.where(col >= row, both, turned)
    other = jnp.where(col == row, diagonal, jnp.where(col > row, turned, both))
    pair = jnp.concatenate([gram / cells, other / snaps], axis=1)
    eliminate(pair, 8 if rank % 8 == 0 else 1, save)
    factors_ref[0] = jnp.where(col >= row, upper_ref[:, :rank], 0.0)
    factors_ref[1] = jnp.where(col >= row, upper_ref[:, rank:], 0.0)
    leaving = [
        pltpu.make_async_copy(factors_ref.at[i], ref, sems.at[out_ref.shape[0] + i])
        for i, ref in enumerate((r_range_ref, r_corange_ref))
    ]
    for copy in leaving:
        copy.start()
    high, low = split(jnp.where(col <= row, lower_ref[:, :rank], 0.0))
    left = jnp.concatenate([high, high, low], axis=1)
    own, comps, _, columns = out_ref.shape
    width = comps * columns
    copies = []
    runs = chunks(lax.axis_index("win"), own)
    for offset, count in runs:
        for r in range(count):
            at = len(copies)
            right = stack_ref[:, at * width : (at + 1) * width]
            value = jnp.dot(left, right, preferred_element_type=F32)
            for c in range(comps):
                out_ref[at, c] = value[:, c * columns : (c + 1) * columns]
            copies.append(pltpu.make_async_copy(out_ref.at[at], q_ref.at[offset + r], sems.at[at]))
            copies[-1].start()
    for copy in copies:
        copy.wait()
    for copy in leaving:
        copy.wait()


def finish(gram, stack, shape, cells, snaps):
    rank = shape[2]
    square = jax.ShapeDtypeStruct((rank, rank), F32)
    return pl.pallas_call(
        lambda *refs: finish_kernel(cells, snaps, *refs),
        out_shape=[jax.ShapeDtypeStruct(shape, F32), square, square],
        in_specs=vmem(2),
        out_specs=[pl.BlockSpec(memory_space=pl.ANY)] * 3,
        scratch_shapes=[
            *[pltpu.VMEM((rank, 2 * rank), F32)] * 2,
            pltpu.VMEM((2, rank, rank), F32),
            pltpu.VMEM(shape, F32),
            pltpu.SemaphoreType.DMA((shape[0] + 2,)),
        ],
        compiler_params=small(16),
        name="finish",
    )(gram, stack)


def swapped(edges):
    count = lax.axis_size("space")
    across = [(i, i + 1) for i in range(1, count - 1, 2)]
    within = [(i, i + 1) for i in range(0, count - 1, 2)]
    far = lax.ppermute(edges[0], "space", across + [(j, i) for i, j in across])
    near = lax.ppermute(edges[1], "space", within + [(j, i) for i, j in within])
    return far, near


def body(snapshots, metrics, range_test, corange_test):
    space, win = lax.axis_size("space"), lax.axis_size("win")
    snaps, comps, tile, columns = snapshots.shape
    rank = range_test.shape[1]
    turned = jnp.transpose(snapshots, (1, 2, 0, 3))
    far, near = swapped(edges_of(turned))
    fields = inner_fields(turned, metrics)
    tests = jnp.transpose(corange_test, (1, 2, 0, 3))
    early, tests = lax.optimization_barrier((early_sketch(fields, range_test.T, win), tests))
    send, edges = sketch_of(turned, fields, far, near, metrics, range_test.T, win)
    got = [[], []]
    for which, rows in enumerate((early, send)):
        for d in range(1, win):
            ring = [(i, (i + d) % win) for i in range(win)]
            got[which].append(lax.ppermute(rows[d - 1], "win", ring))
    projection, own = project(fields, edges, tests, range_test.T, win)
    shares = projection.reshape(space, snaps // 2 // space, 2 * rank)
    shares = lax.all_to_all(shares, "space", 0, 0, tiled=True)
    stack, gram = grams_of(own, jnp.stack(got[0]), jnp.stack(got[1]), shares)
    gram = total_over_all(gram)
    q_turned, r_range, r_corange = finish(
        gram, stack, own.shape, comps * tile * space * columns, snaps * win
    )
    return (jnp.transpose(q_turned, (0, 2, 1, 3)), r_range, r_corange)


def solution(mesh):
    placed = (
        P("win", None, "space", None),
        P(None, "space", None),
        P("win", None),
        P(None, None, "space", None),
    )
    return jax.shard_map(
        body,
        mesh=mesh,
        in_specs=placed,
        out_specs=(P(("space", "win"), None, None, None), P(), P()),
        check_vma=False,
    )
```
